256 devices in a mesh: ctx: 16 (over y, x), tp: 8 (over z), dp: 2 (over core).
Axes of the slice: x: 4, y: 4, z: 8, core: 2. Of those that a mesh axis runs over, the one named last changes fastest.
Arguments:
- query_latent: bfloat16 [2, 2048, 32768], P('dp', 'ctx', 'tp'), may hold values from -120 to 120
- query_rotary: bfloat16 [2, 2048, 4096], P('dp', 'ctx', 'tp'), may hold values from -6 to 6
- key_latent: bfloat16 [2, 2048, 512], P('dp', 'ctx'), may hold values from -6 to 6
- key_rotary: bfloat16 [2, 2048, 64], P('dp', 'ctx'), may hold values from -6 to 6
- value_up: bfloat16 [64, 512, 128], P('tp', 'ctx'), may hold values from -0.25 to 0.25
- out_proj: bfloat16 [64, 128, 3584], P('tp', None, 'ctx'), may hold values from -0.0625 to 0.0625
- residual: bfloat16 [2, 2048, 3584], P('dp', ('ctx', 'tp')), may hold values from -0.59765625 to 0.59765625
- norm_gain: float32 [3584], replicated, may hold values from 0.1 to 1.9
- gate_proj: bfloat16 [128, 3584, 1024], P(('ctx', 'tp'), 'dp'), may hold values from -0.09375 to 0.09375
- up_proj: bfloat16 [128, 3584, 1024], P(('ctx', 'tp'), 'dp'), may hold values from -0.09375 to 0.09375
- down_proj: bfloat16 [128, 1024, 3584], P(('ctx', 'tp'), 'dp'), may hold values from -0.1875 to 0.1875
- expert_ids: int32 [2, 2048, 8], P('dp', ('ctx', 'tp')), may hold values from 0 to 127, all different within a row; in each aligned block of 16 rows (0 to 15, 16 to 31, ..., all dimensions but the last counted through in order) at most 2 rows name the same one
- route_score: float32 [2, 2048, 8], P('dp', ('ctx', 'tp')), may hold values from 0.05 to 1
- out_grad: bfloat16 [2, 2048, 3584], P('dp', ('ctx', 'tp')), may hold values from -6 to 6
Outputs:
- layer_out: bfloat16 [2, 2048, 3584], P('dp', ('ctx', 'tp'))
- resid_grad: bfloat16 [2, 2048, 3584], P('dp', ('ctx', 'tp'))
- score_grad: float32 [2, 2048, 8], P('dp', ('ctx', 'tp'))
The draws below stay inside these ranges and needn't reach their ends.
Inputs may be any that keep to these rules, and one draw needn't show every extreme that they name: `expert_ids`: each token names 8 different experts. In each aligned block of 16 tokens of one sequence no expert is named by more than 2 tokens, a bound that some block reaches.
All inputs are finite; a program needn't handle non-finite values.
Results may differ from the reference program's by a relative error of at most 0.034.
Values may be sent and summed in bfloat16 or wider, within the bound.
A program may use at most 128 MiB of HBM per device.

```python
import math
import jax
import jax.numpy as jnp
import numpy as np
from jax import lax

D = 3584
HID = 1024
LAT = 512
ROPE = 64
VD = 128
TOPK = 8
HEADS = 64
EXPERTS = 128
SEQ = 2048
BATCH = 2
TOK_DEV = 16
CAP = 2


def draw_query_latent(key, part):
    first_key = jax.random.fold_in(jax.random.fold_in(key, 11), 0)
    base = jnp.clip(jax.random.normal(first_key, (BATCH, SEQ, HEADS, LAT), jnp.float32), -4.0, 4.0)
    return base.reshape(BATCH, SEQ, HEADS * LAT).astype(jnp.bfloat16)


def level_of(stream_key, dims, cuts, low, high):
    def one(position, blocks):
        steps = jax.random.uniform(jax.random.fold_in(jax.random.fold_in(stream_key, 6), position), (blocks,), jnp.float32, low / len(cuts), high / len(cuts))
        return jnp.repeat(jnp.exp(steps), dims[position] // blocks).reshape((-1,) + (1,) * (len(dims) - position - 1))

    gain = one(*cuts[0])
    for cut in cuts[1:]:
        gain = gain * one(*cut)
    return gain


def shared_out(rng, own, number, rows, amount, top, most, skew):
    sequence = jax.random.permutation(rng, amount)
    crowded, ordinary = portions_of(amount, rows * top, most, skew, True), portions_of(amount, rows * top, most, skew, False)
    places = jnp.arange(amount)

    def named(lengths, offset_by):
        used = int((lengths > 0).sum())
        fixed = max(1, used // 4)
        passed = fixed + (places - fixed + offset_by * (used - fixed)) % max(1, amount - fixed)
        return jnp.zeros((amount,), jnp.int32).at[sequence[jnp.where(places < fixed, places, passed)]].set(jnp.asarray(lengths, jnp.int32))

    lengths = jnp.where(number % 4 == 0, named(crowded, number // 4), named(ordinary, number - number // 4 - 1))
    mixed = jax.random.permutation(jax.random.fold_in(own, 3), amount)
    source_of, receiver = mixed[0:amount // 2 * 2:2], mixed[1:amount // 2 * 2:2]
    margin = jnp.minimum(lengths[source_of] - 1, most - lengths[receiver]) // 2
    margin = jnp.where((source_of == sequence[0]) | (receiver == sequence[0]) | (lengths[receiver] == 0), 0, jnp.maximum(margin, 0))
    passed = jax.random.randint(jax.random.fold_in(own, 4), (amount // 2,), 0, 1 << 20) % (margin + 1)
    lengths = lengths.at[source_of].add(-passed).at[receiver].add(passed)
    labels = jnp.searchsorted(jnp.cumsum(lengths), jnp.arange(rows * top), side="right").astype(jnp.int32)
    grid = labels.reshape(top, rows).T
    grid = grid[jax.random.permutation(jax.random.fold_in(own, 1), rows)]
    offset_by = jax.random.randint(jax.random.fold_in(own, 2), (rows, 1), 0, top)
    return jnp.take_along_axis(grid, (jnp.arange(top)[None, :] + offset_by) % top, axis=1)


def portions_of(amount, total, bound, skew, full):
    weights = [(1 << 20) // math.isqrt(grade ** skew) + 1 for grade in range(1, amount + 1)]
    largest = bound if full else min(bound, max(-(-total // amount), total * weights[0] // sum(weights)))
    least = 1 if total - largest >= amount - 1 else 0
    given, rest = [largest] + [least] * (amount - 1), total - largest - least * (amount - 1)
    while rest > 0:
        candidates = [i for i in range(1, amount) if given[i] < largest] or [i for i in range(1, amount) if given[i] < bound]
        mass, left = sum([weights[i] for i in candidates]), rest
        for i in candidates:
            more = min(bound - given[i], max(1, left * weights[i] // mass), rest)
            given[i] = given[i] + more
            rest = rest - more
    return np.array(given)


def centred(key, extent, spread, reach, shards=(), held_as=jnp.bfloat16):
    drawn = jax.random.normal(key, extent, jnp.float32) * spread
    if len(shards) > 0:
        drawn = level_of(key, extent, shards, -0.22, 0.18) * drawn
    return jnp.clip(drawn, min=-reach, max=reach).astype(held_as)


def setup_inputs(seed: int = 0) -> dict:
    streams_of = jax.random.split(jax.random.key(seed), 15)
    query_latent = draw_query_latent(jax.random.fold_in(streams_of[14], 71), 0)
    query_rotary = centred(streams_of[1], (BATCH, SEQ, HEADS * ROPE), 1.0, 6.0, ((0, 2), (1, 16), (2, 8)))
    key_latent = centred(streams_of[2], (BATCH, SEQ, LAT), 1.0, 6.0, ((0, 2), (1, 16)))
    key_rotary = centred(streams_of[3], (BATCH, SEQ, ROPE), 1.0, 6.0, ((0, 2), (1, 16)))
    value_up = centred(streams_of[4], (HEADS, LAT, VD), LAT ** -0.5, 0.25, ((0, 8), (1, 16)))
    out_proj = centred(streams_of[5], (HEADS, VD, D), (HEADS * VD) ** -0.5, 0.0625, ((0, 8), (2, 16)))
    residual = centred(streams_of[6], (BATCH, SEQ, D), 0.1, 0.59765625, ((0, 2), (1, 128)))
    norm_gain = jnp.clip(1.0 + 0.18 * jax.random.normal(streams_of[7], (D,), jnp.float32), 0.1, 1.9)
    gate_proj = centred(streams_of[8], (EXPERTS, D, HID), D ** -0.5, 0.09375, ((0, 128), (1, 2)))
    up_proj = centred(streams_of[9], (EXPERTS, D, HID), D ** -0.5, 0.09375, ((0, 128), (1, 2)))
    down_proj = centred(streams_of[10], (EXPERTS, HID, D), HID ** -0.5, 0.1875, ((0, 128), (1, 2)))
    expert_ids_keys = jax.random.split(jax.random.fold_in(streams_of[11], 1), BATCH * SEQ // TOK_DEV)
    expert_ids_turns = jax.random.permutation(jax.random.fold_in(streams_of[11], 3), BATCH * SEQ // TOK_DEV)
    expert_ids = jax.vmap(lambda own, number: shared_out(jax.random.fold_in(streams_of[11], 2), own, number, TOK_DEV, EXPERTS, TOPK, CAP, 2))(expert_ids_keys, expert_ids_turns).reshape((BATCH, SEQ, TOPK))
    route_score = jnp.clip(jnp.exp(math.log(1.0) - 2.9957323 * jax.random.uniform(streams_of[12], (BATCH, SEQ, TOPK), jnp.float32) ** level_of(streams_of[12], (BATCH, SEQ, TOPK), ((0, 2), (1, 128)), -0.2, 0.2)), 0.05, 1.0)
    out_grad = centred(streams_of[13], (BATCH, SEQ, D), 1.0, 6.0, ((0, 2), (1, 128)))
    return dict(query_latent=query_latent, query_rotary=query_rotary, key_latent=key_latent, key_rotary=key_rotary, value_up=value_up, out_proj=out_proj, residual=residual, norm_gain=norm_gain, gate_proj=gate_proj, up_proj=up_proj, down_proj=down_proj, expert_ids=expert_ids, route_score=route_score, out_grad=out_grad)


route_scale = 2.5
norm_eps = 1e-06

def rms_scale(rows_in, norm_gain):
    inverse = lax.rsqrt(lax.optimization_barrier(jnp.mean(rows_in * rows_in, axis=-1, keepdims=True)) + norm_eps)
    return rows_in * inverse * norm_gain

def expert_pass(rows_u, rows_g, gate_w, up_w, down_w):
    act_a = jnp.dot(rows_u, gate_w, preferred_element_type=jnp.float32)
    act_b = jnp.dot(rows_u, up_w, preferred_element_type=jnp.float32)
    gated_act = jax.nn.silu(act_a)
    hidden = (gated_act * act_b).astype(jnp.bfloat16)
    result = jnp.dot(hidden, down_w, preferred_element_type=jnp.float32).astype(jnp.bfloat16)
    d_hidden = jnp.dot(rows_g, down_w.T, preferred_element_type=jnp.float32)
    sigmoid_a = jax.nn.sigmoid(act_a)
    slope_a = sigmoid_a * (1.0 + act_a * (1.0 - sigmoid_a))
    d_gate = (d_hidden * act_b * slope_a).astype(jnp.bfloat16)
    d_up = (d_hidden * gated_act).astype(jnp.bfloat16)
    d_rows = jnp.dot(d_gate, gate_w.T, preferred_element_type=jnp.float32) + jnp.dot(d_up, up_w.T, preferred_element_type=jnp.float32)
    return (result, d_rows.astype(jnp.bfloat16))

def reference(query_latent, query_rotary, key_latent, key_rotary, value_up, out_proj, residual, norm_gain, gate_proj, up_proj, down_proj, expert_ids, route_score, out_grad):
    scale = (VD + ROPE) ** (-0.5)
    positions = jnp.arange(SEQ, dtype=jnp.int32)
    causal = positions[None, :] <= positions[:, None]
    attn_list = []
    for replica in range(BATCH):
        keys_lat = key_latent[replica]
        keys_rot = key_rotary[replica]
        queries = query_latent[replica].reshape(SEQ, HEADS, LAT).transpose(1, 0, 2)
        rotary = query_rotary[replica].reshape(SEQ, HEADS, ROPE).transpose(1, 0, 2)

        def one_head(operands):
            query_head, rotary_head, value_map = operands
            scores = jnp.dot(query_head, keys_lat.T, preferred_element_type=jnp.float32)
            scores = scores + jnp.dot(rotary_head, keys_rot.T, preferred_element_type=jnp.float32)
            scores = jnp.where(causal, scores * scale, -1e+30)
            row_top = lax.optimization_barrier(jnp.max(scores, axis=1, keepdims=True))
            exp_terms = jnp.where(causal, jnp.exp(scores - row_top), 0.0)
            row_total = lax.optimization_barrier(jnp.sum(exp_terms, axis=1, keepdims=True))
            latent_out = (jnp.dot(exp_terms.astype(jnp.bfloat16), keys_lat, preferred_element_type=jnp.float32) / row_total).astype(jnp.bfloat16)
            return jnp.dot(latent_out, value_map, preferred_element_type=jnp.float32).astype(jnp.bfloat16)
        head_out = lax.map(one_head, (queries, rotary, value_up))
        attn_list.append(jnp.einsum('hsv,hvd->sd', head_out.astype(jnp.float32), out_proj.astype(jnp.float32), precision=lax.Precision.HIGHEST))
    attn = jnp.stack(attn_list)
    hidden_sum = residual.astype(jnp.float32) + attn
    normed = rms_scale(hidden_sum, norm_gain).astype(jnp.bfloat16)
    sources = SEQ // TOK_DEV
    slot_width = BATCH * sources * CAP
    route_ids = expert_ids.reshape(BATCH, sources, TOK_DEV * TOPK)
    onehot = (route_ids[..., None] == jnp.arange(EXPERTS, dtype=jnp.int32)).astype(jnp.int32)
    slot_index = lax.optimization_barrier(jnp.sum((jnp.cumsum(onehot, axis=2) - onehot) * onehot, axis=3))
    replica_index = jnp.arange(BATCH, dtype=jnp.int32)[:, None, None]
    source_index = jnp.arange(sources, dtype=jnp.int32)[None, :, None]
    destination = (route_ids * slot_width + replica_index * (sources * CAP) + source_index * CAP + slot_index).reshape(-1).astype(jnp.int32)
    rows_u = jnp.repeat(normed, TOPK, axis=1).reshape(-1, D)
    rows_g = jnp.repeat(out_grad, TOPK, axis=1).reshape(-1, D)
    buffer_u = jnp.zeros((EXPERTS * slot_width, D), jnp.bfloat16).at[destination].set(rows_u).reshape(EXPERTS, slot_width, D)
    buffer_g = jnp.zeros((EXPERTS * slot_width, D), jnp.bfloat16).at[destination].set(rows_g).reshape(EXPERTS, slot_width, D)
    served = lax.map(lambda packed: expert_pass(*packed), (buffer_u, buffer_g, gate_proj, up_proj, down_proj))
    route_out = served[0].reshape(-1, D)[destination].reshape(BATCH, SEQ, TOPK, D).astype(jnp.float32)
    route_grad = served[1].reshape(-1, D)[destination].reshape(BATCH, SEQ, TOPK, D).astype(jnp.float32)
    score_total = lax.optimization_barrier(jnp.sum(route_score, axis=2, keepdims=True))
    route_weight = route_scale * route_score / score_total
    mixed_out = hidden_sum + jnp.einsum('bsk,bskd->bsd', route_weight, route_out, precision=lax.Precision.HIGHEST)
    layer_out = mixed_out.astype(jnp.bfloat16)
    grad_rows = out_grad.astype(jnp.float32)
    weight_grad = jnp.einsum('bsd,bskd->bsk', grad_rows, route_out, precision=lax.Precision.HIGHEST)
    d_normed = jnp.einsum('bsk,bskd->bsd', route_weight, route_grad, precision=lax.Precision.HIGHEST)
    unused, pullback = jax.vjp(lambda rows_in: rms_scale(rows_in, norm_gain), hidden_sum)
    resid_grad = (grad_rows + pullback(d_normed)[0]).astype(jnp.bfloat16)
    score_grad = route_scale / score_total * (weight_grad - lax.optimization_barrier(jnp.sum(weight_grad * route_score, axis=2, keepdims=True)) / score_total)
    return (layer_out, resid_grad, score_grad)
```

```python
import functools

import jax
import jax.numpy as jnp
from jax import lax
from jax.experimental import pallas as pl
from jax.experimental.pallas import tpu as pltpu
from jax.sharding import PartitionSpec as P

MESH = pl.DeviceIdType.MESH
f32 = jnp.float32
bf16 = jnp.bfloat16
route_scale = 2.5
norm_eps = 1e-06
CAP = 2


def remote(src, dst, send_sem, recv_sem, device):
    return pltpu.make_async_remote_copy(
        src_ref=src, dst_ref=dst, send_sem=send_sem, recv_sem=recv_sem, device_id=device, device_id_type=MESH
    )


def each_peer(n, fn):
    def body(off, carry):
        fn(off)
        return carry

    lax.fori_loop(1, n, body, 0)


def each(lo, hi, fn):
    def body(i, carry):
        fn(i)
        return carry

    lax.fori_loop(lo, hi, body, 0)


def nt(a, b):
    return lax.dot_general(a, b, (((1,), (1,)), ((), ())), preferred_element_type=f32)


def nn(a, b):
    return lax.dot_general(a, b, (((1,), (0,)), ((), ())), preferred_element_type=f32)


def tn(a, b):
    return lax.dot_general(a, b, (((0,), (0,)), ((), ())), preferred_element_type=f32)


def attn_kernel(
    C, T,
    ql, qr, kl, kr, vs, os_, res, gain, gw, uw, dw,
    hs_o, nm_o, go, uo, do,
    qbuf, kbuf, sbuf, vbuf, obuf, lat, heads, part, rsb,
    w_ss, w_rs, k_ss, k_rs, v_ss, v_rs, o_ss, o_rs, sv_ss, sv_rs, so_ss, so_rs, r_ss, r_rs,
):
    c, t, d = lax.axis_index("ctx"), lax.axis_index("tp"), lax.axis_index("dp")
    rows = ql.shape[0]
    H, LR, VD = vs.shape
    LAT = kl.shape[1]
    ROPE = kr.shape[1]
    KW = kbuf.shape[1]
    OC = os_.shape[2]
    OH = OC // 2
    Hh = H // 2
    tok, D = res.shape
    scale = (VD + ROPE) ** (-0.5)
    sib = {"dp": 1 - d}

    bar = pltpu.get_barrier_semaphore()
    each_peer(C, lambda o: pl.semaphore_signal(bar, inc=1, device_id={"ctx": lax.rem(c + o, C)}, device_id_type=MESH))
    each_peer(T, lambda o: pl.semaphore_signal(bar, inc=1, device_id={"tp": lax.rem(t + o, T)}, device_id_type=MESH))
    pl.semaphore_signal(bar, inc=1, device_id=sib, device_id_type=MESH)

    my_keys = pl.ds(pl.multiple_of(c * rows, rows), rows)
    kbuf[my_keys, 0:LAT] = kl[...]
    kbuf[my_keys, LAT:KW] = jnp.concatenate([kr[...], jnp.zeros((rows, KW - LAT - ROPE), bf16)], axis=1)
    pl.semaphore_wait(bar, C + T - 1)

    def key_rows(i):
        return kbuf.at[pl.ds(pl.multiple_of(i * rows, rows), rows)]

    each(c + 1, C, lambda j: remote(key_rows(c), key_rows(c), k_ss.at[j], k_rs.at[c], {"ctx": j}).start())

    swaps = [remote(a, b, w_ss.at[i], w_rs.at[i], sib) for i, (a, b) in enumerate(((gw, go), (uw, uo), (dw, do)))]
    for s in swaps:
        s.start()

    eye = (
        lax.broadcasted_iota(jnp.int32, (OC, OC), 0) == lax.broadcasted_iota(jnp.int32, (OC, OC), 1)
    ).astype(bf16)
    obuf[pl.ds(pl.multiple_of(c * OC, OC), OC), :] = nt(eye, os_[...].reshape(H * VD, OC)).astype(bf16)
    vbuf[:, pl.ds(pl.multiple_of(c * LR, LR), LR), :] = vs[...]

    def v_part(owner, half):
        return vbuf.at[pl.ds(half * Hh, Hh), pl.ds(pl.multiple_of(owner * LR, LR), LR), :]

    def o_part(owner, half):
        return obuf.at[pl.ds(pl.multiple_of(owner * OC + half * OH, OH), OH), :]

    def send_vo(off):
        p = lax.rem(c + off, C)
        remote(o_part(c, d), o_part(c, d), o_ss.at[p], o_rs.at[c], {"ctx": p}).start()
        remote(v_part(c, d), v_part(c, d), v_ss.at[p], v_rs.at[c], {"ctx": p}).start()

    each_peer(C, send_vo)

    def blank(j):
        kbuf[pl.ds(pl.multiple_of(j * rows, rows), rows), :] = jnp.zeros((rows, KW), bf16)

    each(c + 1, C, blank)
    for h in range(H):
        qbuf[h * rows : (h + 1) * rows, 0:LAT] = ql[:, h * LAT : (h + 1) * LAT]
        qbuf[h * rows : (h + 1) * rows, LAT:KW] = jnp.concatenate(
            [qr[:, h * ROPE : (h + 1) * ROPE], jnp.zeros((rows, KW - LAT - ROPE), bf16)], axis=1
        )

    each(0, c, lambda j: remote(key_rows(j), key_rows(j), k_ss.at[j], k_rs.at[j], {"ctx": j}).wait_recv())

    S = C * rows
    NB = 4 if S % 4 == 0 else 1
    SN = S // NB
    MB = 2 * rows

    def attend(i):
        r = pl.ds(pl.multiple_of(i * MB, MB), MB)
        q = qbuf[r, :]
        qpos = c * rows + lax.rem(lax.broadcasted_iota(jnp.int32, (MB, SN), 0), rows)
        kpos = lax.broadcasted_iota(jnp.int32, (MB, SN), 1)
        top = jnp.full((MB, 1), -1e30, f32)
        for n in range(NB):
            s = nt(q, kbuf[n * SN : (n + 1) * SN, :]) * scale
            s = jnp.where(kpos + n * SN <= qpos, s, -1e30)
            sbuf[:, n * SN : (n + 1) * SN] = s
            top = jnp.maximum(top, jnp.max(s, axis=1, keepdims=True))
        total = jnp.zeros((MB, 1), f32)
        acc = jnp.zeros((MB, LAT), f32)
        for n in range(NB):
            p = jnp.exp(sbuf[:, n * SN : (n + 1) * SN] - top)
            total = total + jnp.sum(p, axis=1, keepdims=True)
            acc = acc + nn(p.astype(bf16), kbuf[n * SN : (n + 1) * SN, 0:LAT])
        lat[r, :] = (acc / total).astype(bf16)

    each(0, H // 2, attend)

    def relay(off):
        p = lax.rem(c + C - off, C)
        remote(o_part(p, d), o_part(p, d), o_ss.at[p], o_rs.at[p], {"ctx": p}).wait_recv()
        remote(o_part(p, d), o_part(p, d), so_ss.at[p], so_rs.at[p], sib).start()
        remote(v_part(p, d), v_part(p, d), v_ss.at[p], v_rs.at[p], {"ctx": p}).wait_recv()
        remote(v_part(p, d), v_part(p, d), sv_ss.at[p], sv_rs.at[p], sib).start()

    each_peer(C, relay)

    def relayed(off):
        p = lax.rem(c + C - off, C)
        remote(o_part(p, 1 - d), o_part(p, 1 - d), so_ss.at[p], so_rs.at[p], sib).wait_recv()
        remote(v_part(p, 1 - d), v_part(p, 1 - d), sv_ss.at[p], sv_rs.at[p], sib).wait_recv()

    each_peer(C, relayed)

    for h in range(H):
        heads[:, h * VD : (h + 1) * VD] = nn(lat[h * rows : (h + 1) * rows, :], vbuf[h]).astype(bf16)

    PN = 512 if D % 512 == 0 else D

    def project(n):
        cols = pl.ds(pl.multiple_of(n * PN, PN), PN)
        part[:, :, cols] = nt(heads[...], obuf[cols, :]).astype(bf16).reshape(T, tok, PN)

    each(0, D // PN, project)

    def send_part(off):
        p = lax.rem(t + off, T)
        remote(part.at[p], rsb.at[t], r_ss.at[p], r_rs.at[t], {"tp": p}).start()

    each_peer(T, send_part)
    rsb[t] = part[t]

    def got_part(off):
        p = lax.rem(t + T - off, T)
        remote(part.at[p], rsb.at[p], r_ss.at[p], r_rs.at[p], {"tp": p}).wait_recv()

    each_peer(T, got_part)
    hs = rsb[0].astype(f32)
    for i in range(1, T):
        hs = hs + rsb[i].astype(f32)
    hs = hs + res[...].astype(f32)
    hs_o[...] = hs
    inv = lax.rsqrt(jnp.mean(hs * hs, axis=1, keepdims=True) + norm_eps)
    nm_o[...] = (hs * inv * gain[...]).astype(bf16)

    each(c + 1, C, lambda j: remote(key_rows(c), key_rows(c), k_ss.at[j], k_rs.at[c], {"ctx": j}).wait_send())

    def sent(off):
        p = lax.rem(c + off, C)
        remote(o_part(c, d), o_part(c, d), o_ss.at[p], o_rs.at[c], {"ctx": p}).wait_send()
        remote(v_part(c, d), v_part(c, d), v_ss.at[p], v_rs.at[c], {"ctx": p}).wait_send()
        remote(o_part(p, d), o_part(p, d), so_ss.at[p], so_rs.at[p], sib).wait_send()
        remote(v_part(p, d), v_part(p, d), sv_ss.at[p], sv_rs.at[p], sib).wait_send()

    each_peer(C, sent)

    def part_sent(off):
        p = lax.rem(t + off, T)
        remote(part.at[p], rsb.at[t], r_ss.at[p], r_rs.at[t], {"tp": p}).wait_send()

    each_peer(T, part_sent)
    for s in swaps:
        s.wait()


def moe_kernel(
    C, T, K, ND, NR,
    u, g, meta, hs, gain, gw, uw, dw, go, uo, do,
    lo_o, rg_o, sg_o,
    gs, us, ds_, zu, zg, zm, su, sg, au, ag, act, ro, rd, rw, bo, bd, bw, po, pd, pw, fo, fd, fw,
    wl, z_ss, z_rs, x_ss, x_rs, b_ss, b_rs, bw_ss, bw_rs, y_ss, y_rs, yw_ss, yw_rs,
):
    c, t, d = lax.axis_index("ctx"), lax.axis_index("tp"), lax.axis_index("dp")
    tok, D = u.shape
    DH = gw.shape[0]
    HH = dw.shape[0]
    HID = 2 * HH
    SL = CAP * T
    NT = T * tok
    NS = C * SL
    CD, CR = D // ND, D // NR

    loads = []
    for i, (own, other, dst, n) in enumerate(((dw, do, ds_, HH), (gw, go, gs, DH), (uw, uo, us, DH))):
        loads.append(pltpu.make_async_copy(own, dst.at[pl.ds(pl.multiple_of(d * n, n), n)], wl.at[i, 0]))
        loads.append(pltpu.make_async_copy(other, dst.at[pl.ds(pl.multiple_of((1 - d) * n, n), n)], wl.at[i, 1]))
    for s in loads:
        s.start()

    bar = pltpu.get_barrier_semaphore()
    each_peer(C, lambda o: pl.semaphore_signal(bar, inc=1, device_id={"ctx": lax.rem(c + o, C)}, device_id_type=MESH))
    each_peer(T, lambda o: pl.semaphore_signal(bar, inc=1, device_id={"tp": lax.rem(t + o, T)}, device_id_type=MESH))
    zu[t] = u[...]
    zg[t] = g[...]
    zm[t] = meta[...]
    pl.semaphore_wait(bar, C + T - 2)

    zs = (zm, zg, zu)
    for i, z in enumerate(zs):
        each_peer(
            T,
            lambda o: remote(
                z.at[t], z.at[t], z_ss.at[i, lax.rem(t + o, T)], z_rs.at[i, t], {"tp": lax.rem(t + o, T)}
            ).start(),
        )

    def z_wait(i):
        def one(off):
            p = lax.rem(t + T - off, T)
            remote(zs[i].at[p], zs[i].at[p], z_ss.at[i, p], z_rs.at[i, p], {"tp": p}).wait_recv()

        each_peer(T, one)

    z_wait(0)
    m = zm[...].reshape(NT, zm.shape[2])
    lane = lax.broadcasted_iota(jnp.int32, (NT, NS), 1)
    wanted = (lax.div(lane, SL) * T + t).astype(f32)
    slot = lax.rem(lane, SL).astype(f32)
    scores = [m[:, K + k : K + k + 1] for k in range(K)]
    total = scores[0]
    for k in range(1, K):
        total = total + scores[k]
    hit = [(m[:, k : k + 1] == wanted).astype(f32) for k in range(K)]
    match = hit[0]
    weight = hit[0] * (route_scale * scores[0] / total)
    for k in range(1, K):
        match = match + hit[k]
        weight = weight + hit[k] * (route_scale * scores[k] / total)
    below = (
        lax.broadcasted_iota(jnp.int32, (NT, NT), 1) < lax.broadcasted_iota(jnp.int32, (NT, NT), 0)
    ).astype(bf16)
    rank = nn(below, match.astype(bf16))
    pick = jnp.where(rank == slot, match, 0.0)
    place = pick.astype(bf16)
    weight = weight * pick
    w_hi = weight.astype(bf16)
    w_lo = (weight - w_hi.astype(f32)).astype(bf16)

    xs = ((zg, sg, ag), (zu, su, au))

    def dispatch(a):
        z, s_, r_ = xs[a]

        def chunk(n):
            cols = pl.ds(pl.multiple_of(n * CD, CD), CD)
            s_[:, :, cols] = tn(place, z[:, :, cols].reshape(NT, CD)).astype(bf16).reshape(C, SL, CD)

            def send(off):
                p = lax.rem(c + off, C)
                remote(
                    s_.at[p, :, cols], r_.at[c, :, cols], x_ss.at[a * ND + n, p], x_rs.at[a * ND + n, c], {"ctx": p}
                ).start()

            each_peer(C, send)
            r_[c, :, cols] = s_[c, :, cols]

        each(0, ND, chunk)

    def arrived(a, n):
        z, s_, r_ = xs[a]
        cols = pl.ds(pl.multiple_of(n * CD, CD), CD)

        def one(off):
            p = lax.rem(c + C - off, C)
            remote(
                s_.at[p, :, cols], r_.at[p, :, cols], x_ss.at[a * ND + n, p], x_rs.at[a * ND + n, p], {"ctx": p}
            ).wait_recv()

        each_peer(C, one)
        return cols

    z_wait(1)
    dispatch(0)
    z_wait(2)
    dispatch(1)

    loads[0].wait()
    loads[1].wait()
    act[2] = jnp.zeros((NS, HID), f32)

    def d_hidden(n):
        cols = arrived(0, n)
        act[2] += nt(ag[:, :, cols].reshape(NS, CD), ds_[:, cols])

    each(0, ND, d_hidden)
    for i in range(2, 6):
        loads[i].wait()
    act[0] = jnp.zeros((NS, HID), f32)
    act[1] = jnp.zeros((NS, HID), f32)

    def gate_up(n):
        cols = arrived(1, n)
        x = au[:, :, cols].reshape(NS, CD)
        act[0] += nn(x, gs[cols, :])
        act[1] += nn(x, us[cols, :])

    each(0, ND, gate_up)
    a_, b_, dh = act[0], act[1], act[2]
    sig = jax.nn.sigmoid(a_)
    gated = a_ * sig
    hidden = (gated * b_).astype(bf16)
    d_gate = (dh * b_ * (sig * (1.0 + a_ * (1.0 - sig)))).astype(bf16)
    d_up = (dh * gated).astype(bf16)

    backs = ((ro, bo), (rd, bd))

    def send_back(a, n, cols):
        s_, r_ = backs[a]

        def send(off):
            p = lax.rem(c + off, C)
            remote(
                s_.at[p, :, cols], r_.at[c, :, cols], b_ss.at[a * NR + n, p], b_rs.at[a * NR + n, c], {"ctx": p}
            ).start()

        each_peer(C, send)
        r_[c, :, cols] = s_[c, :, cols]

    def result(n, wg):
        cols = pl.ds(pl.multiple_of(n * CR, CR), CR)
        y = nn(hidden, ds_[:, cols]).astype(bf16)
        ro[:, :, cols] = y.reshape(C, SL, CR)
        send_back(0, n, cols)
        return wg + jnp.sum(y.astype(f32) * ag[:, :, cols].reshape(NS, CR).astype(f32), axis=1, keepdims=True)

    wg = lax.fori_loop(0, NR, result, jnp.zeros((NS, 1), f32))
    rw[...] = jnp.broadcast_to(wg, (NS, rw.shape[2])).reshape(rw.shape)

    def send_w(off):
        p = lax.rem(c + off, C)
        remote(rw.at[p], bw.at[c], bw_ss.at[p], bw_rs.at[c], {"ctx": p}).start()

    each_peer(C, send_w)
    bw[c] = rw[c]

    def grads(n):
        cols = pl.ds(pl.multiple_of(n * CR, CR), CR)
        y = nt(d_gate, gs[cols, :]) + nt(d_up, us[cols, :])
        rd[:, :, cols] = y.astype(bf16).reshape(C, SL, CR)
        send_back(1, n, cols)

    each(0, NR, grads)

    sums = ((po, fo), (pd, fd))

    def combine(a):
        s_, r_ = backs[a]
        q_, e_ = sums[a]

        def chunk(n):
            cols = pl.ds(pl.multiple_of(n * CR, CR), CR)

            def one(off):
                p = lax.rem(c + C - off, C)
                remote(
                    s_.at[p, :, cols], r_.at[p, :, cols], b_ss.at[a * NR + n, p], b_rs.at[a * NR + n, p], {"ctx": p}
                ).wait_recv()

            each_peer(C, one)
            x = r_[:, :, cols].reshape(NS, CR)
            q_[:, :, cols] = (nn(w_hi, x) + nn(w_lo, x)).astype(bf16).reshape(T, tok, CR)

            def send(off):
                p = lax.rem(t + off, T)
                remote(
                    q_.at[p, :, cols], e_.at[t, :, cols], y_ss.at[a * NR + n, p], y_rs.at[a * NR + n, t], {"tp": p}
                ).start()

            each_peer(T, send)
            e_[t, :, cols] = q_[t, :, cols]

        each(0, NR, chunk)

    combine(0)

    def got_w(off):
        p = lax.rem(c + C - off, C)
        remote(rw.at[p], bw.at[p], bw_ss.at[p], bw_rs.at[p], {"ctx": p}).wait_recv()

    each_peer(C, got_w)
    wcol = bw[...].reshape(NS, bw.shape[2])
    wlane = lax.broadcasted_iota(jnp.int32, (NT, bw.shape[2]), 1)
    wgk = jnp.zeros((NT, bw.shape[2]), f32)
    for k in range(K):
        v = lax.dot_general(
            hit[k] * pick, wcol, (((1,), (0,)), ((), ())),
            preferred_element_type=f32, precision=lax.Precision.HIGHEST,
        )
        wgk = jnp.where(wlane == k, v, wgk)
    pw[...] = wgk.reshape(pw.shape)

    def send_pw(off):
        p = lax.rem(t + off, T)
        remote(pw.at[p], fw.at[t], yw_ss.at[p], yw_rs.at[t], {"tp": p}).start()

    each_peer(T, send_pw)
    fw[t] = pw[t]

    combine(1)

    def got(a):
        q_, e_ = sums[a]

        def chunk(n):
            cols = pl.ds(pl.multiple_of(n * CR, CR), CR)

            def one(off):
                p = lax.rem(t + T - off, T)
                remote(
                    q_.at[p, :, cols], e_.at[p, :, cols], y_ss.at[a * NR + n, p], y_rs.at[a * NR + n, p], {"tp": p}
                ).wait_recv()

            each_peer(T, one)

        each(0, NR, chunk)

    def total_of(e_):
        v = e_[0].astype(f32)
        for i in range(1, T):
            v = v + e_[i].astype(f32)
        return v

    h = hs[...]
    got(0)
    lo_o[...] = (h + total_of(fo)).astype(bf16)

    def got_pw(off):
        p = lax.rem(t + T - off, T)
        remote(pw.at[p], fw.at[p], yw_ss.at[p], yw_rs.at[p], {"tp": p}).wait_recv()

    each_peer(T, got_pw)
    wgt = total_of(fw)[:, 0:K]
    sc = meta[:, K : 2 * K]
    st = jnp.sum(sc, axis=1, keepdims=True)
    sg_o[...] = route_scale / st * (wgt - jnp.sum(wgt * sc, axis=1, keepdims=True) / st)

    got(1)
    dn = total_of(fd) * gain[...]
    inv = lax.rsqrt(jnp.mean(h * h, axis=1, keepdims=True) + norm_eps)
    proj = jnp.mean(dn * h, axis=1, keepdims=True)
    rg_o[...] = (g[...].astype(f32) + inv * dn - h * (inv * inv * inv * proj)).astype(bf16)

    for i, z in enumerate(zs):
        each_peer(
            T,
            lambda o: remote(
                z.at[t], z.at[t], z_ss.at[i, lax.rem(t + o, T)], z_rs.at[i, t], {"tp": lax.rem(t + o, T)}
            ).wait_send(),
        )

    def drain_x(off):
        p = lax.rem(c + off, C)
        remote(rw.at[p], bw.at[c], bw_ss.at[p], bw_rs.at[c], {"ctx": p}).wait_send()
        for a in range(2):
            def disp(n):
                cols = pl.ds(pl.multiple_of(n * CD, CD), CD)
                remote(
                    xs[a][1].at[p, :, cols], xs[a][2].at[c, :, cols], x_ss.at[a * ND + n, p], x_rs.at[a * ND + n, c],
                    {"ctx": p},
                ).wait_send()

            each(0, ND, disp)

            def back(n):
                cols = pl.ds(pl.multiple_of(n * CR, CR), CR)
                remote(
                    backs[a][0].at[p, :, cols], backs[a][1].at[c, :, cols], b_ss.at[a * NR + n, p],
                    b_rs.at[a * NR + n, c], {"ctx": p},
                ).wait_send()

            each(0, NR, back)

    each_peer(C, drain_x)

    def drain_z(off):
        p = lax.rem(t + off, T)
        remote(pw.at[p], fw.at[t], yw_ss.at[p], yw_rs.at[t], {"tp": p}).wait_send()
        for a in range(2):
            def back(n):
                cols = pl.ds(pl.multiple_of(n * CR, CR), CR)
                remote(
                    sums[a][0].at[p, :, cols], sums[a][1].at[t, :, cols], y_ss.at[a * NR + n, p],
                    y_rs.at[a * NR + n, t], {"tp": p},
                ).wait_send()

            each(0, NR, back)

    each_peer(T, drain_z)


VM = pl.BlockSpec(memory_space=pltpu.VMEM)
ANY = pl.BlockSpec(memory_space=pl.ANY)
LANES = 128


def per_device(
    C, T,
    query_latent, query_rotary, key_latent, key_rotary, value_up, out_proj, residual, norm_gain,
    gate_proj, up_proj, down_proj, expert_ids, route_score, out_grad,
):
    rows = query_latent.shape[1]
    H, LR, VD = value_up.shape
    LAT, ROPE = key_latent.shape[2], key_rotary.shape[2]
    KW = LAT + LANES
    tok, D = residual.shape[1:]
    OC = out_proj.shape[2]
    K = expert_ids.shape[2]
    DH, HID = gate_proj.shape[1:]
    HH = down_proj.shape[1]
    gain = norm_gain.reshape(1, D)
    gate_w, up_w, down_w = gate_proj[0], up_proj[0], down_proj[0]
    dma = pltpu.SemaphoreType.DMA
    shape = jax.ShapeDtypeStruct

    hs, normed, go, uo, do = pl.pallas_call(
        functools.partial(attn_kernel, C, T),
        name="attention",
        out_shape=(
            shape((tok, D), f32), shape((tok, D), bf16),
            shape((DH, HID), bf16), shape((DH, HID), bf16), shape((HH, D), bf16),
        ),
        in_specs=[VM] * 8 + [ANY] * 3,
        out_specs=(VM, VM, ANY, ANY, ANY),
        scratch_shapes=[
            pltpu.VMEM((H * rows, KW), bf16),
            pltpu.VMEM((C * rows, KW), bf16),
            pltpu.VMEM((2 * rows, C * rows), f32),
            pltpu.VMEM((H, LAT, VD), bf16),
            pltpu.VMEM((D, H * VD), bf16),
            pltpu.VMEM((H * rows, LAT), bf16),
            pltpu.VMEM((rows, H * VD), bf16),
            pltpu.VMEM((T, tok, D), bf16),
            pltpu.VMEM((T, tok, D), bf16),
            dma((3,)), dma((3,)),
        ] + [dma((C,))] * 10 + [dma((T,))] * 2,
        compiler_params=pltpu.CompilerParams(
            collective_id=0, has_side_effects=True, vmem_limit_bytes=56 * 1024 * 1024
        ),
    )(
        query_latent[0], query_rotary[0], key_latent[0], key_rotary[0], value_up, out_proj, residual[0], gain,
        gate_w, up_w, down_w,
    )

    meta = jnp.concatenate(
        [expert_ids[0].astype(f32), route_score[0], jnp.zeros((tok, LANES - 2 * K), f32)], axis=1
    )
    SL = CAP * T
    NS = C * SL
    ND, NR = 2, 4
    xy = (C, SL, D)
    zz = (T, tok, D)
    layer_out, resid_grad, score_grad = pl.pallas_call(
        functools.partial(moe_kernel, C, T, K, ND, NR),
        name="experts",
        out_shape=(shape((tok, D), bf16), shape((tok, D), bf16), shape((tok, K), f32)),
        in_specs=[VM] * 5 + [ANY] * 6,
        out_specs=(VM, VM, VM),
        scratch_shapes=[
            pltpu.VMEM((D, HID), bf16), pltpu.VMEM((D, HID), bf16), pltpu.VMEM((HID, D), bf16),
            pltpu.VMEM(zz, bf16), pltpu.VMEM(zz, bf16), pltpu.VMEM((T, tok, LANES), f32),
            pltpu.VMEM(xy, bf16), pltpu.VMEM(xy, bf16), pltpu.VMEM(xy, bf16), pltpu.VMEM(xy, bf16),
            pltpu.VMEM((3, NS, HID), f32),
            pltpu.VMEM(xy, bf16), pltpu.VMEM(xy, bf16), pltpu.VMEM((C, SL, LANES), f32),
            pltpu.VMEM(xy, bf16), pltpu.VMEM(xy, bf16), pltpu.VMEM((C, SL, LANES), f32),
            pltpu.VMEM(zz, bf16), pltpu.VMEM(zz, bf16), pltpu.VMEM((T, tok, LANES), f32),
            pltpu.VMEM(zz, bf16), pltpu.VMEM(zz, bf16), pltpu.VMEM((T, tok, LANES), f32),
            dma((3, 2)),
            dma((3, T)), dma((3, T)),
            dma((2 * ND, C)), dma((2 * ND, C)),
            dma((2 * NR, C)), dma((2 * NR, C)),
            dma((C,)), dma((C,)),
            dma((2 * NR, T)), dma((2 * NR, T)),
            dma((T,)), dma((T,)),
        ],
        compiler_params=pltpu.CompilerParams(
            collective_id=1, has_side_effects=True, vmem_limit_bytes=60 * 1024 * 1024
        ),
    )(normed, out_grad[0], meta, hs, gain, gate_w, up_w, down_w, go, uo, do)
    return (layer_out[None], resid_grad[None], score_grad[None])


def solution(mesh):
    return jax.shard_map(
        functools.partial(per_device, mesh.shape["ctx"], mesh.shape["tp"]),
        mesh=mesh,
        in_specs=(
            P("dp", "ctx", "tp"),
            P("dp", "ctx", "tp"),
            P("dp", "ctx", None),
            P("dp", "ctx", None),
            P("tp", "ctx", None),
            P("tp", None, "ctx"),
            P("dp", ("ctx", "tp"), None),
            P(),
            P(("ctx", "tp"), "dp", None),
            P(("ctx", "tp"), "dp", None),
            P(("ctx", "tp"), "dp", None),
            P("dp", ("ctx", "tp"), None),
            P("dp", ("ctx", "tp"), None),
            P("dp", ("ctx", "tp"), None),
        ),
        out_specs=(
            P("dp", ("ctx", "tp"), None),
            P("dp", ("ctx", "tp"), None),
            P("dp", ("ctx", "tp"), None),
        ),
        check_vma=False,
    )
```

```python
import functools
import math

import jax
import jax.numpy as jnp
from jax import lax
from jax.experimental import pallas as pl
from jax.experimental.pallas import tpu as pltpu
from jax.sharding import PartitionSpec as P

MESH = pl.DeviceIdType.MESH
f32 = jnp.float32
bf16 = jnp.bfloat16
route_scale = 2.5
norm_eps = 1e-06
CAP = 2
LANES = 128


def remote(src, dst, send_sem, recv_sem, device):
    return pltpu.make_async_remote_copy(
        src_ref=src, dst_ref=dst, send_sem=send_sem, recv_sem=recv_sem, device_id=device, device_id_type=MESH
    )


def each(lo, hi, fn):
    def body(i, carry):
        fn(i)
        return carry

    lax.fori_loop(lo, hi, body, 0)


def nt(a, b):
    return lax.dot_general(a, b, (((1,), (1,)), ((), ())), preferred_element_type=f32)


def nn(a, b):
    return lax.dot_general(a, b, (((1,), (0,)), ((), ())), preferred_element_type=f32)


def tn(a, b):
    return lax.dot_general(a, b, (((0,), (0,)), ((), ())), preferred_element_type=f32)


def identity(n):
    return (lax.broadcasted_iota(jnp.int32, (n, n), 0) == lax.broadcasted_iota(jnp.int32, (n, n), 1)).astype(bf16)


def row_of(ref):
    return jnp.concatenate([ref[i : i + 1, :] for i in range(ref.shape[0])], axis=1)


def tour(n):
    if n == 4:
        return [(1, 0), (0, 1), (3, 0), (0, 3), (1, 1), (3, 3), (1, 3), (3, 1), (2, 0), (0, 2), (2, 1), (1, 2),
                (2, 3), (3, 2), (2, 2)]
    return [(i % n, i // n) for i in range(1, n * n)]


def main_kernel(
    C, T, K, ND, NR,
    ql, qr, kl, krt, vs, ost, res, gain, g, meta, gw, uw, dw,
    hs_o, so_o, dn_o, wg_o,
    qbuf, kbuf, vbuf, obuf, us, ds_, heads, part, rsb, zm, zg, zu, sx, ag, au, act, ab, place, wts,
    ro, rd, rw, bo, bd, bw, pd, pw, fo, fd, fw,
    wl, w_ss, w_rs, k_ss, k_rs, v_ss, v_rs, o_ss, o_rs, sv_ss, sv_rs, so_ss, so_rs, r_ss, r_rs,
    zm_ss, zm_rs, zg_ss, zg_rs, zu_ss, zu_rs, xg_ss, xg_rs, xu_ss, xu_rs, b_ss, b_rs, bw_ss, bw_rs,
    y_ss, y_rs, yw_ss, yw_rs, ready,
):
    c, t, d = lax.axis_index("ctx"), lax.axis_index("tp"), lax.axis_index("dp")
    NX = math.isqrt(C)
    rows = ql.shape[0]
    H, LR, VD = vs.shape
    LAT = kl.shape[1]
    ROPE = krt.shape[0]
    KW = kbuf.shape[1]
    OC = ost.shape[1]
    OH = OC // 2
    Hh = H // 2
    tok, D = res.shape
    DH, HH = gw.shape[0], dw.shape[0]
    HID = 2 * HH
    SL = CAP * T
    NT = T * tok
    NS = C * SL
    CD, CG, CR = D // ND, D // 2, D // NR
    scale = (VD + ROPE) ** (-0.5)
    sib = {"dp": 1 - d}
    gs = obuf

    row, col = lax.div(c, NX), lax.rem(c, NX)
    a = col * (1 - d) + row * d
    b = row * (1 - d) + col * d
    sa, sb = 1 + (NX - 1) * d, NX - (NX - 1) * d

    def at(da, db):
        return lax.rem(a + da, NX) * sa + lax.rem(b + db, NX) * sb

    hops = tour(NX)

    def to_xy(fn):
        for da, db in hops:
            fn(at(da, db))

    def from_xy(fn):
        each(1, C, lambda off: fn(lax.rem(c + C - off, C)))

    def to_z(fn):
        each(1, T, lambda off: fn(lax.rem(t + off, T)))

    def from_z(fn):
        each(1, T, lambda off: fn(lax.rem(t + T - off, T)))

    bar = pltpu.get_barrier_semaphore()
    from_xy(lambda p: pl.semaphore_signal(bar, inc=1, device_id={"ctx": p}, device_id_type=MESH))
    to_z(lambda p: pl.semaphore_signal(bar, inc=1, device_id={"tp": p}, device_id_type=MESH))
    pl.semaphore_signal(bar, inc=1, device_id=sib, device_id_type=MESH)

    def half_rows(ref, who, n):
        return ref.at[pl.ds(pl.multiple_of(who * n, n), n)]

    own_d = pltpu.make_async_copy(dw, half_rows(ds_, d, HH), wl.at[0])
    own_u = pltpu.make_async_copy(uw, half_rows(us, d, DH), wl.at[1])
    own_g = pltpu.make_async_copy(gw, half_rows(gs, d, DH), wl.at[2])
    own_d.start()
    own_u.start()
    swap_d = remote(dw, half_rows(ds_, d, HH), w_ss.at[0], w_rs.at[0], sib)
    swap_u = remote(uw, half_rows(us, d, DH), w_ss.at[1], w_rs.at[1], sib)
    swap_g = remote(gw, half_rows(gs, d, DH), w_ss.at[2], w_rs.at[2], sib)

    def key_rows(i):
        return kbuf.at[pl.ds(pl.multiple_of(i * rows, rows), rows)]

    my_keys = pl.ds(pl.multiple_of(c * rows, rows), rows)
    kbuf[my_keys, 0:LAT] = kl[...]
    kr = tn(krt[...], identity(ROPE)).astype(bf16)
    kbuf[my_keys, LAT:KW] = jnp.concatenate([kr, jnp.zeros((rows, KW - LAT - ROPE), bf16)], axis=1)
    zm[t] = meta[...]
    zg[t] = g[...]
    pl.semaphore_wait(bar, C + T - 1)

    def send_keys(p):
        @pl.when(p > c)
        def _():
            remote(key_rows(c), key_rows(c), k_ss.at[p], k_rs.at[c], {"ctx": p}).start()

    to_xy(send_keys)
    to_z(lambda p: remote(zm.at[t], zm.at[t], zm_ss.at[p], zm_rs.at[t], {"tp": p}).start())
    to_z(lambda p: remote(zg.at[t], zg.at[t], zg_ss.at[p], zg_rs.at[t], {"tp": p}).start())
    swap_d.start()
    swap_u.start()

    for h in range(H):
        obuf[pl.ds(pl.multiple_of(c * OC, OC), OC), h * VD : (h + 1) * VD] = ost[h]
    vbuf[:, pl.ds(pl.multiple_of(c * LR, LR), LR), :] = vs[...]

    def v_part(owner, half):
        return vbuf.at[pl.ds(half * Hh, Hh), pl.ds(pl.multiple_of(owner * LR, LR), LR), :]

    def o_part(owner, half):
        return obuf.at[pl.ds(pl.multiple_of(owner * OC + half * OH, OH), OH), :]

    def vo(owner, s, dest):
        return (
            remote(o_part(owner, d), o_part(owner, d), o_ss.at[s], o_rs.at[owner], {"ctx": dest}),
            remote(v_part(owner, d), v_part(owner, d), v_ss.at[s], v_rs.at[owner], {"ctx": dest}),
        )

    def vo_relay(owner, half):
        return (
            remote(o_part(owner, half), o_part(owner, half), so_ss.at[owner], so_rs.at[owner], sib),
            remote(v_part(owner, half), v_part(owner, half), sv_ss.at[owner], sv_rs.at[owner], sib),
        )

    def start(copies):
        for x in copies:
            x.start()

    def wait_recv(copies):
        for x in copies:
            x.wait_recv()

    def wait_send(copies):
        for x in copies:
            x.wait_send()

    def blank(j):
        kbuf[pl.ds(pl.multiple_of(j * rows, rows), rows), :] = jnp.zeros((rows, KW), bf16)

    each(c + 1, C, blank)
    for h in range(H):
        qbuf[h * rows : (h + 1) * rows, 0:LAT] = ql[:, h * LAT : (h + 1) * LAT]
        qbuf[h * rows : (h + 1) * rows, LAT:KW] = jnp.concatenate(
            [qr[:, h * ROPE : (h + 1) * ROPE], jnp.zeros((rows, KW - LAT - ROPE), bf16)], axis=1
        )

    each(0, c, lambda j: remote(key_rows(j), key_rows(j), k_ss.at[j], k_rs.at[j], {"ctx": j}).wait_recv())

    for o in range(1, NX):
        start(vo(c, o, at(o, 0)))
    for o in range(1, NX):
        start(vo(c, NX + o, at(0, o)))

    def pass_on(i):
        owner = lax.rem(a + NX - i, NX) * sa + b * sb
        wait_recv(vo(owner, 0, owner))
        for o in range(1, NX):
            start(vo(owner, NX * (i + 1) + o, at(0, o)))
        start(vo_relay(owner, d))

    S = C * rows
    NB = 4
    SN = S // NB
    MB = 2 * rows

    def sc(n):
        return act.at[n // 2, 0:MB, (n % 2) * SN : (n % 2 + 1) * SN]

    def attend(i):
        @pl.when(jnp.logical_and(i > 0, i < NX))
        def _():
            pass_on(i)

        r = pl.ds(pl.multiple_of(i * MB, MB), MB)
        q = qbuf[r, :]
        qpos = c * rows + lax.rem(lax.broadcasted_iota(jnp.int32, (MB, SN), 0), rows)
        kpos = lax.broadcasted_iota(jnp.int32, (MB, SN), 1)
        top = jnp.full((MB, 1), -1e30, f32)
        for n in range(NB):
            s = nt(q, kbuf[n * SN : (n + 1) * SN, :]) * scale
            s = jnp.where(kpos + n * SN <= qpos, s, -1e30)
            sc(n)[...] = s
            top = jnp.maximum(top, jnp.max(s, axis=1, keepdims=True))
        total = jnp.zeros((MB, 1), f32)
        acc = jnp.zeros((MB, LAT), f32)
        for n in range(NB):
            p = jnp.exp(sc(n)[...] - top)
            total = total + jnp.sum(p, axis=1, keepdims=True)
            acc = acc + nn(p.astype(bf16), kbuf[n * SN : (n + 1) * SN, 0:LAT])
        qbuf[r, 0:LAT] = (acc / total).astype(bf16)

    each(0, H // 2, attend)

    from_z(lambda p: remote(zm.at[p], zm.at[p], zm_ss.at[p], zm_rs.at[p], {"tp": p}).wait_recv())
    lane = lax.broadcasted_iota(jnp.int32, (NT, NS), 1)
    wanted = (lax.div(lane, SL) * T + t).astype(f32)

    def hit(k):
        return (zm[...].reshape(NT, LANES)[:, k : k + 1] == wanted).astype(f32)

    m = zm[...].reshape(NT, LANES)
    total = m[:, K : K + 1]
    for k in range(1, K):
        total = total + m[:, K + k : K + k + 1]
    match = hit(0)
    weight = match * (route_scale * m[:, K : K + 1] / total)
    for k in range(1, K):
        h_ = hit(k)
        match = match + h_
        weight = weight + h_ * (route_scale * m[:, K + k : K + k + 1] / total)
    below = (
        lax.broadcasted_iota(jnp.int32, (NT, NT), 1) < lax.broadcasted_iota(jnp.int32, (NT, NT), 0)
    ).astype(bf16)
    rank = nn(below, match.astype(bf16))
    pick = jnp.where(rank == lax.rem(lane, SL).astype(f32), match, 0.0)
    place[...] = pick.astype(bf16)
    weight = weight * pick
    w_hi = weight.astype(bf16)
    wts[0] = w_hi
    wts[1] = (weight - w_hi.astype(f32)).astype(bf16)

    from_z(lambda p: remote(zg.at[p], zg.at[p], zg_ss.at[p], zg_rs.at[p], {"tp": p}).wait_recv())

    def g_cols(n):
        return pl.ds(pl.multiple_of(n * CG, CG), CG)

    def place_g(n):
        cols = g_cols(n)
        sx[:, :, cols] = tn(place[...], zg[:, :, cols].reshape(NT, CG)).astype(bf16).reshape(C, SL, CG)
        ag[c, :, cols] = sx[c, :, cols]

    each(0, 2, place_g)

    def relay(bo_):
        def one(ai):
            owner = lax.rem(a + ai, NX) * sa + lax.rem(b + NX - bo_, NX) * sb
            wait_recv(vo(owner, 0, owner))
            start(vo_relay(owner, d))

        each(0, NX, one)

    for o in (1, 3, 2) if NX == 4 else range(1, NX):
        relay(o)

    def xg(n, p, q):
        cols = g_cols(n)
        return remote(sx.at[p, :, cols], ag.at[q, :, cols], xg_ss.at[n, p], xg_rs.at[n, q], {"ctx": p})

    each(0, 2, lambda n: to_xy(lambda p: xg(n, p, c).start()))

    from_xy(lambda p: wait_recv(vo_relay(p, 1 - d)))

    for h in range(H):
        heads[:, h * VD : (h + 1) * VD] = nn(qbuf[h * rows : (h + 1) * rows, 0:LAT], vbuf[h]).astype(bf16)

    PN = 512 if D % 512 == 0 else D

    def project(n):
        cols = pl.ds(pl.multiple_of(n * PN, PN), PN)
        part[:, :, cols] = nt(heads[...], obuf[cols, :]).astype(bf16).reshape(T, tok, PN)

    each(0, D // PN, project)
    to_z(lambda p: remote(part.at[p], rsb.at[t], r_ss.at[p], r_rs.at[t], {"tp": p}).start())
    rsb[t] = part[t]

    def sent_vo(off):
        for o in range(1, NX):
            wait_send(vo(c, NX * off + o, c))

    each(0, NX + 1, sent_vo)
    from_xy(lambda p: wait_send(vo_relay(p, d)))
    pl.semaphore_signal(ready, inc=1, device_id=sib, device_id_type=MESH)
    own_g.start()

    from_z(lambda p: remote(part.at[p], rsb.at[p], r_ss.at[p], r_rs.at[p], {"tp": p}).wait_recv())
    hs = rsb[0].astype(f32)
    for i in range(1, T):
        hs = hs + rsb[i].astype(f32)
    hs = hs + res[...].astype(f32)
    hs_o[...] = hs
    inv = lax.rsqrt(jnp.mean(hs * hs, axis=1, keepdims=True) + norm_eps)
    zu[t] = (hs * inv * row_of(gain)).astype(bf16)

    def u_cols(n):
        return pl.ds(pl.multiple_of(n * CD, CD), CD)

    def z_u(n, p, q):
        cols = u_cols(n)
        return remote(zu.at[q, :, cols], zu.at[q, :, cols], zu_ss.at[n, p], zu_rs.at[n, q], {"tp": p})

    each(0, ND, lambda n: to_z(lambda p: z_u(n, p, t).start()))
    pl.semaphore_wait(ready, 1)
    swap_g.start()
    each(0, 2, lambda n: from_xy(lambda p: xg(n, p, c).wait_send()))

    def x_u(n, p, q):
        cols = u_cols(n)
        return remote(sx.at[p, :, cols], au.at[q, :, cols], xu_ss.at[n, p], xu_rs.at[n, q], {"ctx": p})

    def send_u(n):
        cols = u_cols(n)
        from_z(lambda p: z_u(n, p, p).wait_recv())
        sx[:, :, cols] = tn(place[...], zu[:, :, cols].reshape(NT, CD)).astype(bf16).reshape(C, SL, CD)
        to_xy(lambda p: x_u(n, p, c).start())
        au[c, :, cols] = sx[c, :, cols]

    each(0, ND, send_u)

    own_d.wait()
    swap_d.wait()
    act[2] = jnp.zeros((NS, HID), f32)

    def d_hidden(n):
        from_xy(lambda p: xg(n, p, p).wait_recv())
        cols = g_cols(n)
        act[2] += nt(ag[:, :, cols].reshape(NS, CG), ds_[:, cols])

    each(0, 2, d_hidden)
    own_u.wait()
    swap_u.wait()
    own_g.wait()
    swap_g.wait()
    act[0] = jnp.zeros((NS, HID), f32)
    act[1] = jnp.zeros((NS, HID), f32)

    def gate_up(n):
        from_xy(lambda p: x_u(n, p, p).wait_recv())
        cols = u_cols(n)
        x = au[:, :, cols].reshape(NS, CD)
        act[0] += nn(x, gs[cols, :])
        act[1] += nn(x, us[cols, :])

    each(0, ND, gate_up)

    EB = NS // 4

    def pointwise(i):
        r = pl.ds(pl.multiple_of(i * EB, EB), EB)
        a_, b_, dh = act[0, r, :], act[1, r, :], act[2, r, :]
        sig = jax.nn.sigmoid(a_)
        gated = a_ * sig
        ab[0, r, :] = (gated * b_).astype(bf16)
        ab[1, r, :] = (dh * b_ * (sig * (1.0 + a_ * (1.0 - sig)))).astype(bf16)
        ab[2, r, :] = (dh * gated).astype(bf16)

    each(0, 4, pointwise)

    backs = ((ro, bo), (rd, bd))

    def r_cols(n):
        return pl.ds(pl.multiple_of(n * CR, CR), CR)

    def back(i, n, p, q):
        s_, r_ = backs[i]
        cols = r_cols(n)
        return remote(s_.at[p, :, cols], r_.at[q, :, cols], b_ss.at[i * NR + n, p], b_rs.at[i * NR + n, q], {"ctx": p})

    def w_back(p, q):
        return remote(rw.at[p], bw.at[q], bw_ss.at[p], bw_rs.at[q], {"ctx": p})

    def result(n, wg):
        cols = r_cols(n)
        y = nn(ab[0], ds_[:, cols]).astype(bf16)
        ro[:, :, cols] = y.reshape(C, SL, CR)
        to_xy(lambda p: back(0, n, p, c).start())
        bo[c, :, cols] = ro[c, :, cols]
        return wg + jnp.sum(y.astype(f32) * ag[:, :, cols].reshape(NS, CR).astype(f32), axis=1, keepdims=True)

    wg = lax.fori_loop(0, NR, result, jnp.zeros((NS, 1), f32))
    rw[...] = jnp.broadcast_to(wg, (NS, LANES)).reshape(rw.shape)
    to_xy(lambda p: w_back(p, c).start())
    bw[c] = rw[c]

    def grads(n):
        cols = r_cols(n)
        y = nt(ab[1], gs[cols, :]) + nt(ab[2], us[cols, :])
        rd[:, :, cols] = y.astype(bf16).reshape(C, SL, CR)
        to_xy(lambda p: back(1, n, p, c).start())
        bd[c, :, cols] = rd[c, :, cols]

    each(0, NR, grads)

    to_z(lambda p: remote(part.at[p], rsb.at[t], r_ss.at[p], r_rs.at[t], {"tp": p}).wait_send())
    sums = ((part, fo), (pd, fd))

    def z_back(i, n, p, q):
        s_, r_ = sums[i]
        cols = r_cols(n)
        return remote(s_.at[p, :, cols], r_.at[q, :, cols], y_ss.at[i * NR + n, p], y_rs.at[i * NR + n, q], {"tp": p})

    def w_sum(p, q):
        return remote(pw.at[p], fw.at[q], yw_ss.at[p], yw_rs.at[q], {"tp": p})

    def combine(i):
        def chunk(n):
            cols = r_cols(n)
            from_xy(lambda p: back(i, n, p, p).wait_recv())
            x = backs[i][1][:, :, cols].reshape(NS, CR)
            sums[i][0][:, :, cols] = (nn(wts[0], x) + nn(wts[1], x)).astype(bf16).reshape(T, tok, CR)
            to_z(lambda p: z_back(i, n, p, t).start())
            sums[i][1][t, :, cols] = sums[i][0][t, :, cols]

        each(0, NR, chunk)

    combine(0)
    from_xy(lambda p: w_back(p, p).wait_recv())
    wcol = bw[...].reshape(NS, LANES)
    wlane = lax.broadcasted_iota(jnp.int32, (NT, LANES), 1)
    wgk = jnp.zeros((NT, LANES), f32)
    chosen = place[...].astype(f32)
    for k in range(K):
        v = lax.dot_general(
            hit(k) * chosen, wcol, (((1,), (0,)), ((), ())), preferred_element_type=f32, precision=lax.Precision.HIGHEST
        )
        wgk = jnp.where(wlane == k, v, wgk)
    pw[...] = wgk.reshape(pw.shape)
    to_z(lambda p: w_sum(p, t).start())
    fw[t] = pw[t]
    combine(1)

    def total_of(ref):
        v = ref[0].astype(f32)
        for i in range(1, T):
            v = v + ref[i].astype(f32)
        return v

    each(0, NR, lambda n: from_z(lambda p: z_back(0, n, p, p).wait_recv()))
    so_o[...] = total_of(fo)
    from_z(lambda p: w_sum(p, p).wait_recv())
    wg_o[...] = total_of(fw)

    to_z(lambda p: remote(zm.at[t], zm.at[t], zm_ss.at[p], zm_rs.at[t], {"tp": p}).wait_send())
    to_z(lambda p: remote(zg.at[t], zg.at[t], zg_ss.at[p], zg_rs.at[t], {"tp": p}).wait_send())
    each(0, ND, lambda n: to_z(lambda p: z_u(n, p, t).wait_send()))
    each(0, ND, lambda n: from_xy(lambda p: x_u(n, p, c).wait_send()))
    for i in range(2):
        each(0, NR, lambda n: from_xy(lambda p: back(i, n, p, c).wait_send()))
    from_xy(lambda p: w_back(p, c).wait_send())
    each(c + 1, C, lambda j: remote(key_rows(c), key_rows(c), k_ss.at[j], k_rs.at[c], {"ctx": j}).wait_send())

    each(0, NR, lambda n: from_z(lambda p: z_back(1, n, p, p).wait_recv()))
    dn_o[...] = total_of(fd)
    to_z(lambda p: w_sum(p, t).wait_send())
    for i in range(2):
        each(0, NR, lambda n: to_z(lambda p: z_back(i, n, p, t).wait_send()))


def final_kernel(K, hs, so, dn, wg, g, meta, gain, lo_o, rg_o, sg_o):
    h = hs[...]
    lo_o[...] = (h + so[...]).astype(bf16)
    wgt = wg[:, 0:K]
    sc = meta[:, K : 2 * K]
    st = jnp.sum(sc, axis=1, keepdims=True)
    sg_o[...] = route_scale / st * (wgt - jnp.sum(wgt * sc, axis=1, keepdims=True) / st)
    dng = dn[...] * row_of(gain)
    inv = lax.rsqrt(jnp.mean(h * h, axis=1, keepdims=True) + norm_eps)
    proj = jnp.mean(dng * h, axis=1, keepdims=True)
    rg_o[...] = (g[...].astype(f32) + inv * dng - h * (inv * inv * inv * proj)).astype(bf16)


VM = pl.BlockSpec(memory_space=pltpu.VMEM)
ANY = pl.BlockSpec(memory_space=pl.ANY)


def per_device(
    C, T,
    query_latent, query_rotary, key_latent, key_rotary, value_up, out_proj, residual, norm_gain,
    gate_proj, up_proj, down_proj, expert_ids, route_score, out_grad,
):
    rows = query_latent.shape[1]
    H, LR, VD = value_up.shape
    LAT, ROPE = key_latent.shape[2], key_rotary.shape[2]
    KW = LAT + LANES
    tok, D = residual.shape[1:]
    K = expert_ids.shape[2]
    HID = gate_proj.shape[2]
    SL = CAP * T
    NS = C * SL
    NT = T * tok
    NX = math.isqrt(C)
    ND, NR = 4, 4
    gain = norm_gain.reshape(D // LANES, LANES)
    meta = jnp.concatenate(
        [expert_ids[0].astype(f32), route_score[0], jnp.zeros((tok, LANES - 2 * K), f32)], axis=1
    )
    dma = pltpu.SemaphoreType.DMA
    shape = jax.ShapeDtypeStruct
    vmem = pltpu.VMEM
    xy = (C, SL, D)
    zz = (T, tok, D)

    hs, so, dn, wg = pl.pallas_call(
        functools.partial(main_kernel, C, T, K, ND, NR),
        name="layer",
        out_shape=(shape((tok, D), f32), shape((tok, D), f32), shape((tok, D), f32), shape((tok, LANES), f32)),
        in_specs=[VM] * 10 + [ANY] * 3,
        out_specs=(VM,) * 4,
        scratch_shapes=[
            vmem((H * rows, KW), bf16),
            vmem((C * rows, KW), bf16),
            vmem((H, LAT, VD), bf16),
            vmem((D, H * VD), bf16),
            vmem((D, HID), bf16),
            vmem((HID, D), bf16),
            vmem((rows, H * VD), bf16),
            vmem(zz, bf16), vmem(zz, bf16),
            vmem((T, tok, LANES), f32), vmem(zz, bf16), vmem(zz, bf16),
            vmem(xy, bf16), vmem(xy, bf16), vmem(xy, bf16),
            vmem((3, NS, HID), f32),
            vmem((3, NS, HID), bf16),
            vmem((NT, NS), bf16), vmem((2, NT, NS), bf16),
            vmem(xy, bf16), vmem(xy, bf16), vmem((C, SL, LANES), f32),
            vmem(xy, bf16), vmem(xy, bf16), vmem((C, SL, LANES), f32),
            vmem(zz, bf16), vmem((T, tok, LANES), f32),
            vmem(zz, bf16), vmem(zz, bf16), vmem((T, tok, LANES), f32),
            dma((3,)), dma((3,)), dma((3,)),
            dma((C,)), dma((C,)),
            dma((NX * (NX + 1),)), dma((C,)), dma((NX * (NX + 1),)), dma((C,)),
            dma((C,)), dma((C,)), dma((C,)), dma((C,)),
            dma((T,)), dma((T,)),
            dma((T,)), dma((T,)), dma((T,)), dma((T,)), dma((ND, T)), dma((ND, T)),
            dma((2, C)), dma((2, C)), dma((ND, C)), dma((ND, C)),
            dma((2 * NR, C)), dma((2 * NR, C)), dma((C,)), dma((C,)),
            dma((2 * NR, T)), dma((2 * NR, T)), dma((T,)), dma((T,)),
            pltpu.SemaphoreType.REGULAR,
        ],
        compiler_params=pltpu.CompilerParams(
            collective_id=0, has_side_effects=True, vmem_limit_bytes=60 * 1024 * 1024
        ),
    )(
        query_latent[0], query_rotary[0], key_latent[0], jnp.swapaxes(key_rotary[0], 0, 1), value_up,
        jnp.swapaxes(out_proj, 1, 2), residual[0], gain, out_grad[0], meta, gate_proj[0], up_proj[0], down_proj[0],
    )
    layer_out, resid_grad, score_grad = pl.pallas_call(
        functools.partial(final_kernel, K),
        name="finish",
        out_shape=(shape((tok, D), bf16), shape((tok, D), bf16), shape((tok, K), f32)),
        in_specs=[VM] * 7,
        out_specs=(VM,) * 3,
    )(hs, so, dn, wg, out_grad[0], meta, gain)
    return (layer_out[None], resid_grad[None], score_grad[None])


def solution(mesh):
    return jax.shard_map(
        functools.partial(per_device, mesh.shape["ctx"], mesh.shape["tp"]),
        mesh=mesh,
        in_specs=(
            P("dp", "ctx", "tp"),
            P("dp", "ctx", "tp"),
            P("dp", "ctx", None),
            P("dp", "ctx", None),
            P("tp", "ctx", None),
            P("tp", None, "ctx"),
            P("dp", ("ctx", "tp"), None),
            P(),
            P(("ctx", "tp"), "dp", None),
            P(("ctx", "tp"), "dp", None),
            P(("ctx", "tp"), "dp", None),
            P("dp", ("ctx", "tp"), None),
            P("dp", ("ctx", "tp"), None),
            P("dp", ("ctx", "tp"), None),
        ),
        out_specs=(
            P("dp", ("ctx", "tp"), None),
            P("dp", ("ctx", "tp"), None),
            P("dp", ("ctx", "tp"), None),
        ),
        check_vma=False,
    )
```

```python
import functools
import math

import jax
import jax.numpy as jnp
from jax import lax
from jax.experimental import pallas as pl
from jax.experimental.pallas import tpu as pltpu
from jax.sharding import PartitionSpec as P

MESH = pl.DeviceIdType.MESH
f32 = jnp.float32
bf16 = jnp.bfloat16
route_scale = 2.5
norm_eps = 1e-06
CAP = 2
LANES = 128


def remote(src, dst, send_sem, recv_sem, device):
    return pltpu.make_async_remote_copy(
        src_ref=src, dst_ref=dst, send_sem=send_sem, recv_sem=recv_sem, device_id=device, device_id_type=MESH
    )


def each(lo, hi, fn):
    def body(i, carry):
        fn(i)
        return carry

    lax.fori_loop(lo, hi, body, 0)


def nt(a, b):
    return lax.dot_general(a, b, (((1,), (1,)), ((), ())), preferred_element_type=f32)


def nn(a, b):
    return lax.dot_general(a, b, (((1,), (0,)), ((), ())), preferred_element_type=f32)


def tn(a, b):
    return lax.dot_general(a, b, (((0,), (0,)), ((), ())), preferred_element_type=f32)


def identity(n):
    return (lax.broadcasted_iota(jnp.int32, (n, n), 0) == lax.broadcasted_iota(jnp.int32, (n, n), 1)).astype(bf16)


def row_of(ref):
    return jnp.concatenate([ref[i : i + 1, :] for i in range(ref.shape[0])], axis=1)


def exact_tn(x, y):
    return lax.dot_general(
        x, y, (((0,), (0,)), ((), ())), preferred_element_type=f32, precision=lax.Precision.HIGHEST
    )


def exact_nt(x, y):
    return lax.dot_general(
        x, y, (((1,), (1,)), ((), ())), preferred_element_type=f32, precision=lax.Precision.HIGHEST
    )


def unit_rows(n, first):
    at_row = lax.broadcasted_iota(jnp.int32, (n, LANES), 0) + first
    return (lax.broadcasted_iota(jnp.int32, (n, LANES), 1) == at_row).astype(f32)


def lanes_of(x, first):
    return exact_tn(x, unit_rows(x.shape[0], first))


def tour(n):
    if n == 4:
        return [(1, 0), (0, 1), (3, 0), (0, 3), (1, 1), (3, 3), (1, 3), (3, 1), (2, 0), (0, 2), (2, 1), (1, 2),
                (2, 3), (3, 2), (2, 2)]
    return [(i % n, i // n) for i in range(1, n * n)]


def main_kernel(
    C, T, K, ND, NR,
    ql, qr, kl, krt, vs, ost, res, gain, g, idt, sct, gw, uw, dw,
    hs_o, so_o, dn_o, wg_o,
    qbuf, kbuf, vbuf, obuf, us, ds_, heads, part, rsb, zm, zg, zu, sx, ag, au, act, ab, place, wts,
    ro, rd, rw, bo, bd, bw, pd, pw, fo, fd, fw,
    wl, w_ss, w_rs, k_ss, k_rs, kz_ss, kz_rs, v_ss, v_rs, o_ss, o_rs, sv_ss, sv_rs, so_ss, so_rs, r_ss, r_rs,
    zm_ss, zm_rs, zg_ss, zg_rs, zu_ss, zu_rs, xg_ss, xg_rs, xu_ss, xu_rs, b_ss, b_rs, bw_ss, bw_rs,
    y_ss, y_rs, yw_ss, yw_rs, ready,
):
    c, t, d = lax.axis_index("ctx"), lax.axis_index("tp"), lax.axis_index("dp")
    NX = math.isqrt(C)
    rows = ql.shape[0]
    H, LR, VD = vs.shape
    LAT = kl.shape[1]
    ROPE = krt.shape[0]
    KW = kbuf.shape[1]
    OC = ost.shape[1]
    OH = OC // 2
    Hh = H // 2
    tok, D = res.shape
    DH, HH = gw.shape[0], dw.shape[0]
    HID = 2 * HH
    SL = CAP * T
    NT = T * tok
    NS = C * SL
    CD, CG, CR = D // ND, D // 2, D // NR
    scale = (VD + ROPE) ** (-0.5)
    sib = {"dp": 1 - d}
    gs = obuf

    row, col = lax.div(c, NX), lax.rem(c, NX)
    a = col * (1 - d) + row * d
    b = row * (1 - d) + col * d
    sa, sb = 1 + (NX - 1) * d, NX - (NX - 1) * d

    def at(da, db):
        return lax.rem(a + da, NX) * sa + lax.rem(b + db, NX) * sb

    hops = tour(NX)

    def to_xy(fn):
        for da, db in hops:
            fn(at(da, db))

    def from_xy(fn):
        each(1, C, lambda off: fn(lax.rem(c + C - off, C)))

    def to_z(fn):
        each(1, T, lambda off: fn(lax.rem(t + off, T)))

    def from_z(fn):
        each(1, T, lambda off: fn(lax.rem(t + T - off, T)))

    bar = pltpu.get_barrier_semaphore()
    from_xy(lambda p: pl.semaphore_signal(bar, inc=1, device_id={"ctx": p}, device_id_type=MESH))
    to_z(lambda p: pl.semaphore_signal(bar, inc=1, device_id={"tp": p}, device_id_type=MESH))
    pl.semaphore_signal(bar, inc=1, device_id=sib, device_id_type=MESH)

    def half_rows(ref, who, n):
        return ref.at[pl.ds(pl.multiple_of(who * n, n), n)]

    own_d = pltpu.make_async_copy(dw, half_rows(ds_, d, HH), wl.at[0])
    own_u = pltpu.make_async_copy(uw, half_rows(us, d, DH), wl.at[1])
    own_g = pltpu.make_async_copy(gw, half_rows(gs, d, DH), wl.at[2])
    own_d.start()
    own_u.start()
    swap_d = remote(dw, half_rows(ds_, d, HH), w_ss.at[0], w_rs.at[0], sib)
    swap_u = remote(uw, half_rows(us, d, DH), w_ss.at[1], w_rs.at[1], sib)
    swap_g = remote(gw, half_rows(gs, d, DH), w_ss.at[2], w_rs.at[2], sib)

    HR = rows // 2
    side = lax.rem(t, 2)
    mate = {"tp": t + 1 - 2 * side}

    def key_half(i, h):
        return kbuf.at[pl.ds(pl.multiple_of(i * rows + h * HR, HR), HR)]

    def key_copy(owner, p):
        return remote(key_half(owner, side), key_half(owner, side), k_ss.at[p], k_rs.at[owner], {"ctx": p})

    def key_pass(owner, h):
        return remote(key_half(owner, h), key_half(owner, h), kz_ss.at[owner], kz_rs.at[owner], mate)

    my_keys = pl.ds(pl.multiple_of(c * rows, rows), rows)
    kbuf[my_keys, 0:LAT] = kl[...]
    kr = tn(krt[...], identity(ROPE)).astype(bf16)
    kbuf[my_keys, LAT:KW] = jnp.concatenate([kr, jnp.zeros((rows, KW - LAT - ROPE), bf16)], axis=1)
    zm[t] = lanes_of(idt[...].astype(f32), 0) + lanes_of(sct[...], K)
    zg[t] = g[...]
    for h in range(H):
        obuf[pl.ds(pl.multiple_of(c * OC, OC), OC), h * VD : (h + 1) * VD] = ost[h]
    vbuf[:, pl.ds(pl.multiple_of(c * LR, LR), LR), :] = vs[...]
    pl.semaphore_wait(bar, C + T - 1)


    def v_part(owner, half):
        return vbuf.at[pl.ds(half * Hh, Hh), pl.ds(pl.multiple_of(owner * LR, LR), LR), :]

    def o_part(owner, half):
        return obuf.at[pl.ds(pl.multiple_of(owner * OC + half * OH, OH), OH), :]

    def vo(owner, s, dest):
        return (
            remote(o_part(owner, d), o_part(owner, d), o_ss.at[s], o_rs.at[owner], {"ctx": dest}),
            remote(v_part(owner, d), v_part(owner, d), v_ss.at[s], v_rs.at[owner], {"ctx": dest}),
        )

    def vo_relay(owner, half):
        return (
            remote(o_part(owner, half), o_part(owner, half), so_ss.at[owner], so_rs.at[owner], sib),
            remote(v_part(owner, half), v_part(owner, half), sv_ss.at[owner], sv_rs.at[owner], sib),
        )

    def start(copies):
        for x in copies:
            x.start()

    def wait_recv(copies):
        for x in copies:
            x.wait_recv()

    def wait_send(copies):
        for x in copies:
            x.wait_send()

    for o in range(1, NX):
        start(vo(c, o, at(o, 0)))

    def send_keys(p):
        @pl.when(p > c)
        def _():
            key_copy(c, p).start()

    to_xy(send_keys)
    for o in range(1, NX):
        start(vo(c, NX + o, at(0, o)))
    to_z(lambda p: remote(zm.at[t], zm.at[t], zm_ss.at[p], zm_rs.at[t], {"tp": p}).start())
    swap_d.start()
    swap_u.start()

    def blank(j):
        kbuf[pl.ds(pl.multiple_of(j * rows, rows), rows), :] = jnp.zeros((rows, KW), bf16)

    each(c + 1, C, blank)
    for h in range(H):
        qbuf[h * rows : (h + 1) * rows, 0:LAT] = ql[:, h * LAT : (h + 1) * LAT]
        qbuf[h * rows : (h + 1) * rows, LAT:KW] = jnp.concatenate(
            [qr[:, h * ROPE : (h + 1) * ROPE], jnp.zeros((rows, KW - LAT - ROPE), bf16)], axis=1
        )

    def pass_on(i):
        owner = lax.rem(a + NX - i, NX) * sa + b * sb
        wait_recv(vo(owner, 0, owner))
        for o in range(1, NX):
            start(vo(owner, NX * (i + 1) + o, at(0, o)))
        start(vo_relay(owner, d))

    for i in (1, 3, 2) if NX == 4 else range(1, NX):
        pass_on(i)

    def key_relay(j):
        key_copy(j, j).wait_recv()
        key_pass(j, side).start()

    each(0, c, key_relay)
    to_z(lambda p: remote(zg.at[t], zg.at[t], zg_ss.at[p], zg_rs.at[t], {"tp": p}).start())
    each(0, c, lambda j: key_pass(j, 1 - side).wait_recv())

    S = C * rows
    NB = 4
    SN = S // NB
    MB = 2 * rows

    def sc(n):
        return act.at[n // 2, 0:MB, (n % 2) * SN : (n % 2 + 1) * SN]

    def attend(i):
        r = pl.ds(pl.multiple_of(i * MB, MB), MB)
        q = qbuf[r, :]
        qpos = c * rows + lax.rem(lax.broadcasted_iota(jnp.int32, (MB, SN), 0), rows)
        kpos = lax.broadcasted_iota(jnp.int32, (MB, SN), 1)
        top = jnp.full((MB, 1), -1e30, f32)
        for n in range(NB):
            s = nt(q, kbuf[n * SN : (n + 1) * SN, :]) * scale
            s = jnp.where(kpos + n * SN <= qpos, s, -1e30)
            sc(n)[...] = s
            top = jnp.maximum(top, jnp.max(s, axis=1, keepdims=True))
        total = jnp.zeros((MB, 1), f32)
        acc = jnp.zeros((MB, LAT), f32)
        for n in range(NB):
            p = jnp.exp(sc(n)[...] - top)
            total = total + jnp.sum(p, axis=1, keepdims=True)
            acc = acc + nn(p.astype(bf16), kbuf[n * SN : (n + 1) * SN, 0:LAT])
        qbuf[r, 0:LAT] = (acc / total).astype(bf16)

    each(0, H // 2, attend)

    from_z(lambda p: remote(zm.at[p], zm.at[p], zm_ss.at[p], zm_rs.at[p], {"tp": p}).wait_recv())
    lane = lax.broadcasted_iota(jnp.int32, (NT, NS), 1)
    wanted = (lax.div(lane, SL) * T + t).astype(f32)

    def hit(k):
        return (zm[...].reshape(NT, LANES)[:, k : k + 1] == wanted).astype(f32)

    m = zm[...].reshape(NT, LANES)
    total = m[:, K : K + 1]
    for k in range(1, K):
        total = total + m[:, K + k : K + k + 1]
    match = hit(0)
    weight = match * (route_scale * m[:, K : K + 1] / total)
    for k in range(1, K):
        h_ = hit(k)
        match = match + h_
        weight = weight + h_ * (route_scale * m[:, K + k : K + k + 1] / total)
    below = (
        lax.broadcasted_iota(jnp.int32, (NT, NT), 1) < lax.broadcasted_iota(jnp.int32, (NT, NT), 0)
    ).astype(bf16)
    rank = nn(below, match.astype(bf16))
    pick = jnp.where(rank == lax.rem(lane, SL).astype(f32), match, 0.0)
    place[...] = pick.astype(bf16)
    weight = weight * pick
    w_hi = weight.astype(bf16)
    wts[0] = w_hi
    wts[1] = (weight - w_hi.astype(f32)).astype(bf16)

    from_z(lambda p: remote(zg.at[p], zg.at[p], zg_ss.at[p], zg_rs.at[p], {"tp": p}).wait_recv())

    def g_cols(n):
        return pl.ds(pl.multiple_of(n * CG, CG), CG)

    def place_g(n):
        cols = g_cols(n)
        sx[:, :, cols] = tn(place[...], zg[:, :, cols].reshape(NT, CG)).astype(bf16).reshape(C, SL, CG)
        ag[c, :, cols] = sx[c, :, cols]

    each(0, 2, place_g)

    def relay(bo_):
        def one(ai):
            owner = lax.rem(a + ai, NX) * sa + lax.rem(b + NX - bo_, NX) * sb
            wait_recv(vo(owner, 0, owner))
            start(vo_relay(owner, d))

        each(0, NX, one)

    for o in (1, 3, 2) if NX == 4 else range(1, NX):
        relay(o)

    def xg(n, p, q):
        cols = g_cols(n)
        return remote(sx.at[p, :, cols], ag.at[q, :, cols], xg_ss.at[n, p], xg_rs.at[n, q], {"ctx": p})

    each(0, 2, lambda n: to_xy(lambda p: xg(n, p, c).start()))

    from_xy(lambda p: wait_recv(vo_relay(p, 1 - d)))

    for h in range(H):
        heads[:, h * VD : (h + 1) * VD] = nn(qbuf[h * rows : (h + 1) * rows, 0:LAT], vbuf[h]).astype(bf16)

    def u_cols(n):
        return pl.ds(pl.multiple_of(n * CD, CD), CD)

    def partial(n, p, q):
        cols = u_cols(n)
        return remote(part.at[p, :, cols], rsb.at[q, :, cols], r_ss.at[n, p], r_rs.at[n, q], {"tp": p})

    def project(n):
        cols = u_cols(n)
        part[:, :, cols] = nt(heads[...], obuf[cols, :]).astype(bf16).reshape(T, tok, CD)
        to_z(lambda p: partial(n, p, t).start())
        rsb[t, :, cols] = part[t, :, cols]

    each(0, ND, project)

    def sent_vo(off):
        for o in range(1, NX):
            wait_send(vo(c, NX * off + o, c))

    each(0, NX + 1, sent_vo)
    from_xy(lambda p: wait_send(vo_relay(p, d)))
    pl.semaphore_signal(ready, inc=1, device_id=sib, device_id_type=MESH)
    own_g.start()

    each(0, ND, lambda n: from_z(lambda p: partial(n, p, p).wait_recv()))
    hs = rsb[0].astype(f32)
    for i in range(1, T):
        hs = hs + rsb[i].astype(f32)
    hs = hs + res[...].astype(f32)
    hs_o[...] = hs
    inv = lax.rsqrt(jnp.mean(hs * hs, axis=1, keepdims=True) + norm_eps)
    zu[t] = (hs * inv * row_of(gain)).astype(bf16)

    def z_u(n, p, q):
        cols = u_cols(n)
        return remote(zu.at[q, :, cols], zu.at[q, :, cols], zu_ss.at[n, p], zu_rs.at[n, q], {"tp": p})

    each(0, ND, lambda n: to_z(lambda p: z_u(n, p, t).start()))
    pl.semaphore_wait(ready, 1)
    swap_g.start()
    each(0, 2, lambda n: from_xy(lambda p: xg(n, p, c).wait_send()))

    def x_u(n, p, q):
        cols = u_cols(n)
        return remote(sx.at[p, :, cols], au.at[q, :, cols], xu_ss.at[n, p], xu_rs.at[n, q], {"ctx": p})

    def send_u(n):
        cols = u_cols(n)
        from_z(lambda p: z_u(n, p, p).wait_recv())
        sx[:, :, cols] = tn(place[...], zu[:, :, cols].reshape(NT, CD)).astype(bf16).reshape(C, SL, CD)
        to_xy(lambda p: x_u(n, p, c).start())
        au[c, :, cols] = sx[c, :, cols]

    each(0, ND, send_u)

    own_d.wait()
    swap_d.wait()
    act[2] = jnp.zeros((NS, HID), f32)

    def d_hidden(n):
        from_xy(lambda p: xg(n, p, p).wait_recv())
        cols = g_cols(n)
        act[2] += nt(ag[:, :, cols].reshape(NS, CG), ds_[:, cols])

    each(0, 2, d_hidden)
    own_u.wait()
    swap_u.wait()
    own_g.wait()
    swap_g.wait()
    act[0] = jnp.zeros((NS, HID), f32)
    act[1] = jnp.zeros((NS, HID), f32)

    def gate_up(n):
        from_xy(lambda p: x_u(n, p, p).wait_recv())
        cols = u_cols(n)
        x = au[:, :, cols].reshape(NS, CD)
        act[0] += nn(x, gs[cols, :])
        act[1] += nn(x, us[cols, :])

    each(0, ND, gate_up)

    EB = NS // 4

    def pointwise(i):
        r = pl.ds(pl.multiple_of(i * EB, EB), EB)
        a_, b_, dh = act[0, r, :], act[1, r, :], act[2, r, :]
        sig = jax.nn.sigmoid(a_)
        gated = a_ * sig
        ab[0, r, :] = (gated * b_).astype(bf16)
        ab[1, r, :] = (dh * b_ * (sig * (1.0 + a_ * (1.0 - sig)))).astype(bf16)
        ab[2, r, :] = (dh * gated).astype(bf16)

    each(0, 4, pointwise)

    backs = ((ro, bo), (rd, bd))

    def r_cols(n):
        return pl.ds(pl.multiple_of(n * CR, CR), CR)

    def back(i, n, p, q):
        s_, r_ = backs[i]
        cols = r_cols(n)
        return remote(s_.at[p, :, cols], r_.at[q, :, cols], b_ss.at[i * NR + n, p], b_rs.at[i * NR + n, q], {"ctx": p})

    def w_back(p, q):
        return remote(rw.at[p], bw.at[q], bw_ss.at[p], bw_rs.at[q], {"ctx": p})

    def result(n, wg):
        cols = r_cols(n)
        y = nn(ab[0], ds_[:, cols]).astype(bf16)
        ro[:, :, cols] = y.reshape(C, SL, CR)
        to_xy(lambda p: back(0, n, p, c).start())
        bo[c, :, cols] = ro[c, :, cols]
        return wg + jnp.sum(y.astype(f32) * ag[:, :, cols].reshape(NS, CR).astype(f32), axis=1, keepdims=True)

    wg = lax.fori_loop(0, NR, result, jnp.zeros((NS, 1), f32))
    rw[...] = jnp.broadcast_to(wg, (NS, LANES)).reshape(rw.shape)
    to_xy(lambda p: w_back(p, c).start())
    bw[c] = rw[c]

    def grads(n):
        cols = r_cols(n)
        y = nt(ab[1], gs[cols, :]) + nt(ab[2], us[cols, :])
        rd[:, :, cols] = y.astype(bf16).reshape(C, SL, CR)
        to_xy(lambda p: back(1, n, p, c).start())
        bd[c, :, cols] = rd[c, :, cols]

    each(0, NR, grads)

    each(0, ND, lambda n: to_z(lambda p: partial(n, p, t).wait_send()))
    sums = ((part, fo), (pd, fd))

    def z_back(i, n, p, q):
        s_, r_ = sums[i]
        cols = r_cols(n)
        return remote(s_.at[p, :, cols], r_.at[q, :, cols], y_ss.at[i * NR + n, p], y_rs.at[i * NR + n, q], {"tp": p})

    def w_sum(p, q):
        return remote(pw.at[p], fw.at[q], yw_ss.at[p], yw_rs.at[q], {"tp": p})

    def combine(i):
        def chunk(n):
            cols = r_cols(n)
            from_xy(lambda p: back(i, n, p, p).wait_recv())
            x = backs[i][1][:, :, cols].reshape(NS, CR)
            sums[i][0][:, :, cols] = (nn(wts[0], x) + nn(wts[1], x)).astype(bf16).reshape(T, tok, CR)
            to_z(lambda p: z_back(i, n, p, t).start())
            sums[i][1][t, :, cols] = sums[i][0][t, :, cols]

        each(0, NR, chunk)

    combine(0)
    from_xy(lambda p: w_back(p, p).wait_recv())
    wcol = bw[...].reshape(NS, LANES)
    wlane = lax.broadcasted_iota(jnp.int32, (NT, LANES), 1)
    wgk = jnp.zeros((NT, LANES), f32)
    chosen = place[...].astype(f32)
    for k in range(K):
        v = lax.dot_general(
            hit(k) * chosen, wcol, (((1,), (0,)), ((), ())), preferred_element_type=f32, precision=lax.Precision.HIGHEST
        )
        wgk = jnp.where(wlane == k, v, wgk)
    pw[...] = wgk.reshape(pw.shape)
    to_z(lambda p: w_sum(p, t).start())
    fw[t] = pw[t]
    combine(1)

    def total_of(ref):
        v = ref[0].astype(f32)
        for i in range(1, T):
            v = v + ref[i].astype(f32)
        return v

    each(0, NR, lambda n: from_z(lambda p: z_back(0, n, p, p).wait_recv()))
    so_o[...] = total_of(fo)
    from_z(lambda p: w_sum(p, p).wait_recv())
    wg_o[...] = total_of(fw)

    to_z(lambda p: remote(zm.at[t], zm.at[t], zm_ss.at[p], zm_rs.at[t], {"tp": p}).wait_send())
    to_z(lambda p: remote(zg.at[t], zg.at[t], zg_ss.at[p], zg_rs.at[t], {"tp": p}).wait_send())
    each(0, ND, lambda n: to_z(lambda p: z_u(n, p, t).wait_send()))
    each(0, ND, lambda n: from_xy(lambda p: x_u(n, p, c).wait_send()))
    for i in range(2):
        each(0, NR, lambda n: from_xy(lambda p: back(i, n, p, c).wait_send()))
    from_xy(lambda p: w_back(p, c).wait_send())
    each(c + 1, C, lambda j: key_copy(c, j).wait_send())
    each(0, c, lambda j: key_pass(j, side).wait_send())

    each(0, NR, lambda n: from_z(lambda p: z_back(1, n, p, p).wait_recv()))
    dn_o[...] = total_of(fd)
    to_z(lambda p: w_sum(p, t).wait_send())
    for i in range(2):
        each(0, NR, lambda n: to_z(lambda p: z_back(i, n, p, t).wait_send()))


def final_kernel(K, hs, so, dn, wg, g, sct, gain, lo_o, rg_o, sg_o):
    h = hs[...]
    lo_o[...] = (h + so[...]).astype(bf16)
    wgt = exact_nt(unit_rows(K, 0), wg[...])
    sc = sct[...]
    st = jnp.sum(sc, axis=0, keepdims=True)
    sg_o[...] = route_scale / st * (wgt - jnp.sum(wgt * sc, axis=0, keepdims=True) / st)
    dng = dn[...] * row_of(gain)
    inv = lax.rsqrt(jnp.mean(h * h, axis=1, keepdims=True) + norm_eps)
    proj = jnp.mean(dng * h, axis=1, keepdims=True)
    rg_o[...] = (g[...].astype(f32) + inv * dng - h * (inv * inv * inv * proj)).astype(bf16)


VM = pl.BlockSpec(memory_space=pltpu.VMEM)
ANY = pl.BlockSpec(memory_space=pl.ANY)


def per_device(
    C, T,
    query_latent, query_rotary, key_latent, key_rotary, value_up, out_proj, residual, norm_gain,
    gate_proj, up_proj, down_proj, expert_ids, route_score, out_grad,
):
    rows = query_latent.shape[1]
    H, LR, VD = value_up.shape
    LAT, ROPE = key_latent.shape[2], key_rotary.shape[2]
    KW = LAT + LANES
    tok, D = residual.shape[1:]
    K = expert_ids.shape[2]
    HID = gate_proj.shape[2]
    SL = CAP * T
    NS = C * SL
    NT = T * tok
    NX = math.isqrt(C)
    ND, NR = 4, 4
    gain = norm_gain.reshape(D // LANES, LANES)
    id_t = jnp.swapaxes(expert_ids[0], 0, 1)
    score_t = jnp.swapaxes(route_score[0], 0, 1)
    dma = pltpu.SemaphoreType.DMA
    shape = jax.ShapeDtypeStruct
    vmem = pltpu.VMEM
    xy = (C, SL, D)
    zz = (T, tok, D)

    hs, so, dn, wg = pl.pallas_call(
        functools.partial(main_kernel, C, T, K, ND, NR),
        name="layer",
        out_shape=(shape((tok, D), f32), shape((tok, D), f32), shape((tok, D), f32), shape((tok, LANES), f32)),
        in_specs=[VM] * 11 + [ANY] * 3,
        out_specs=(VM,) * 4,
        scratch_shapes=[
            vmem((H * rows, KW), bf16),
            vmem((C * rows, KW), bf16),
            vmem((H, LAT, VD), bf16),
            vmem((D, H * VD), bf16),
            vmem((D, HID), bf16),
            vmem((HID, D), bf16),
            vmem((rows, H * VD), bf16),
            vmem(zz, bf16), vmem(zz, bf16),
            vmem((T, tok, LANES), f32), vmem(zz, bf16), vmem(zz, bf16),
            vmem(xy, bf16), vmem(xy, bf16), vmem(xy, bf16),
            vmem((3, NS, HID), f32),
            vmem((3, NS, HID), bf16),
            vmem((NT, NS), bf16), vmem((2, NT, NS), bf16),
            vmem(xy, bf16), vmem(xy, bf16), vmem((C, SL, LANES), f32),
            vmem(xy, bf16), vmem(xy, bf16), vmem((C, SL, LANES), f32),
            vmem(zz, bf16), vmem((T, tok, LANES), f32),
            vmem(zz, bf16), vmem(zz, bf16), vmem((T, tok, LANES), f32),
            dma((3,)), dma((3,)), dma((3,)),
            dma((C,)), dma((C,)), dma((C,)), dma((C,)),
            dma((NX * (NX + 1),)), dma((C,)), dma((NX * (NX + 1),)), dma((C,)),
            dma((C,)), dma((C,)), dma((C,)), dma((C,)),
            dma((ND, T)), dma((ND, T)),
            dma((T,)), dma((T,)), dma((T,)), dma((T,)), dma((ND, T)), dma((ND, T)),
            dma((2, C)), dma((2, C)), dma((ND, C)), dma((ND, C)),
            dma((2 * NR, C)), dma((2 * NR, C)), dma((C,)), dma((C,)),
            dma((2 * NR, T)), dma((2 * NR, T)), dma((T,)), dma((T,)),
            pltpu.SemaphoreType.REGULAR,
        ],
        compiler_params=pltpu.CompilerParams(
            collective_id=0, has_side_effects=True, vmem_limit_bytes=60 * 1024 * 1024
        ),
    )(
        query_latent[0], query_rotary[0], key_latent[0], jnp.swapaxes(key_rotary[0], 0, 1), value_up,
        jnp.swapaxes(out_proj, 1, 2), residual[0], gain, out_grad[0], id_t, score_t, gate_proj[0], up_proj[0],
        down_proj[0],
    )
    layer_out, resid_grad, score_grad = pl.pallas_call(
        functools.partial(final_kernel, K),
        name="finish",
        out_shape=(shape((tok, D), bf16), shape((tok, D), bf16), shape((K, tok), f32)),
        in_specs=[VM] * 7,
        out_specs=(VM,) * 3,
    )(hs, so, dn, wg, out_grad[0], score_t, gain)
    return (layer_out[None], resid_grad[None], jnp.swapaxes(score_grad, 0, 1)[None])


def solution(mesh):
    return jax.shard_map(
        functools.partial(per_device, mesh.shape["ctx"], mesh.shape["tp"]),
        mesh=mesh,
        in_specs=(
            P("dp", "ctx", "tp"),
            P("dp", "ctx", "tp"),
            P("dp", "ctx", None),
            P("dp", "ctx", None),
            P("tp", "ctx", None),
            P("tp", None, "ctx"),
            P("dp", ("ctx", "tp"), None),
            P(),
            P(("ctx", "tp"), "dp", None),
            P(("ctx", "tp"), "dp", None),
            P(("ctx", "tp"), "dp", None),
            P("dp", ("ctx", "tp"), None),
            P("dp", ("ctx", "tp"), None),
            P("dp", ("ctx", "tp"), None),
        ),
        out_specs=(
            P("dp", ("ctx", "tp"), None),
            P("dp", ("ctx", "tp"), None),
            P("dp", ("ctx", "tp"), None),
        ),
        check_vma=False,
    )
```

```python
import functools
import math

import jax
import jax.numpy as jnp
from jax import lax
from jax.experimental import pallas as pl
from jax.experimental.pallas import tpu as pltpu
from jax.sharding import PartitionSpec as P

MESH = pl.DeviceIdType.MESH
f32 = jnp.float32
bf16 = jnp.bfloat16
route_scale = 2.5
norm_eps = 1e-06
CAP = 2
LANES = 128


def remote(src, dst, send_sem, recv_sem, device):
    return pltpu.make_async_remote_copy(
        src_ref=src, dst_ref=dst, send_sem=send_sem, recv_sem=recv_sem, device_id=device, device_id_type=MESH
    )


def each(lo, hi, fn):
    def body(i, carry):
        fn(i)
        return carry

    lax.fori_loop(lo, hi, body, 0)


def nt(a, b):
    return lax.dot_general(a, b, (((1,), (1,)), ((), ())), preferred_element_type=f32)


def nn(a, b):
    return lax.dot_general(a, b, (((1,), (0,)), ((), ())), preferred_element_type=f32)


def tn(a, b):
    return lax.dot_general(a, b, (((0,), (0,)), ((), ())), preferred_element_type=f32)


def identity(n):
    return (lax.broadcasted_iota(jnp.int32, (n, n), 0) == lax.broadcasted_iota(jnp.int32, (n, n), 1)).astype(bf16)


def row_of(ref):
    return jnp.concatenate([ref[i : i + 1, :] for i in range(ref.shape[0])], axis=1)


def exact_tn(x, y):
    return lax.dot_general(
        x, y, (((0,), (0,)), ((), ())), preferred_element_type=f32, precision=lax.Precision.HIGHEST
    )


def exact_nt(x, y):
    return lax.dot_general(
        x, y, (((1,), (1,)), ((), ())), preferred_element_type=f32, precision=lax.Precision.HIGHEST
    )


def unit_rows(n, first):
    at_row = lax.broadcasted_iota(jnp.int32, (n, LANES), 0) + first
    return (lax.broadcasted_iota(jnp.int32, (n, LANES), 1) == at_row).astype(f32)


def lanes_of(x, first):
    return exact_tn(x, unit_rows(x.shape[0], first))


def tour(n):
    if n == 4:
        return [(1, 0), (0, 1), (3, 0), (0, 3), (1, 1), (3, 3), (1, 3), (3, 1), (2, 0), (0, 2), (2, 1), (1, 2),
                (2, 3), (3, 2), (2, 2)]
    return [(i % n, i // n) for i in range(1, n * n)]


def main_kernel(
    C, T, K, ND, NR,
    ql, qr, kl, krt, vs, ost, res, gain, g, idt, sct, gw, uw, dw,
    hs_o, so_o, dn_o, wg_o,
    qbuf, kbuf, vbuf, obuf, us, ds_, heads, part, rsb, zm, zg, zu, sx, ag, au, act, ab, place, wts,
    ro, rd, rw, bo, bd, bw, pd, pw, fo, fd, fw,
    wl, w_ss, w_rs, k_ss, k_rs, kz_ss, kz_rs, v_ss, v_rs, o_ss, o_rs, sv_ss, sv_rs, so_ss, so_rs, r_ss, r_rs,
    zm_ss, zm_rs, zg_ss, zg_rs, zu_ss, zu_rs, xg_ss, xg_rs, xu_ss, xu_rs, b_ss, b_rs, bw_ss, bw_rs,
    y_ss, y_rs, yw_ss, yw_rs, ready,
):
    c, t, d = lax.axis_index("ctx"), lax.axis_index("tp"), lax.axis_index("dp")
    NX = math.isqrt(C)
    rows = ql.shape[0]
    H, LR, VD = vs.shape
    LAT = kl.shape[1]
    ROPE = krt.shape[0]
    KW = kbuf.shape[1]
    OC = ost.shape[1]
    OH = OC // 2
    Hh = H // 2
    tok, D = res.shape
    DH, HH = gw.shape[0], dw.shape[0]
    HID = 2 * HH
    SL = CAP * T
    NT = T * tok
    NS = C * SL
    CD, CG, CR = D // ND, D // 2, D // NR
    scale = (VD + ROPE) ** (-0.5)
    sib = {"dp": 1 - d}
    gs = obuf

    row, col = lax.div(c, NX), lax.rem(c, NX)
    a = col * (1 - d) + row * d
    b = row * (1 - d) + col * d
    sa, sb = 1 + (NX - 1) * d, NX - (NX - 1) * d

    def at(da, db):
        return lax.rem(a + da, NX) * sa + lax.rem(b + db, NX) * sb

    hops = tour(NX)

    def to_xy(fn):
        for da, db in hops:
            fn(at(da, db))

    def from_xy(fn):
        each(1, C, lambda off: fn(lax.rem(c + C - off, C)))

    def to_z(fn):
        each(1, T, lambda off: fn(lax.rem(t + off, T)))

    def from_z(fn):
        each(1, T, lambda off: fn(lax.rem(t + T - off, T)))

    bar = pltpu.get_barrier_semaphore()
    from_xy(lambda p: pl.semaphore_signal(bar, inc=1, device_id={"ctx": p}, device_id_type=MESH))
    to_z(lambda p: pl.semaphore_signal(bar, inc=1, device_id={"tp": p}, device_id_type=MESH))
    pl.semaphore_signal(bar, inc=1, device_id=sib, device_id_type=MESH)

    def half_rows(ref, who, n):
        return ref.at[pl.ds(pl.multiple_of(who * n, n), n)]

    own_d = pltpu.make_async_copy(dw, half_rows(ds_, d, HH), wl.at[0])
    own_u = pltpu.make_async_copy(uw, half_rows(us, d, DH), wl.at[1])
    own_g = pltpu.make_async_copy(gw, half_rows(gs, d, DH), wl.at[2])
    own_d.start()
    own_u.start()
    swap_d = remote(dw, half_rows(ds_, d, HH), w_ss.at[0], w_rs.at[0], sib)
    swap_u = remote(uw, half_rows(us, d, DH), w_ss.at[1], w_rs.at[1], sib)
    swap_g = remote(gw, half_rows(gs, d, DH), w_ss.at[2], w_rs.at[2], sib)

    ZR = rows * 3 // 8
    XR = rows - ZR
    side = lax.rem(t, 2)
    mate = {"tp": t + 1 - 2 * side}

    def key_copy(owner, p):
        ref = kbuf.at[pl.ds(pl.multiple_of(owner * rows + side * ZR, math.gcd(rows, ZR)), XR)]
        return remote(ref, ref, k_ss.at[p], k_rs.at[owner], {"ctx": p})

    def key_pass(owner, h):
        ref = kbuf.at[pl.ds(pl.multiple_of(owner * rows + h * XR, math.gcd(rows, XR)), ZR)]
        return remote(ref, ref, kz_ss.at[owner], kz_rs.at[owner], mate)

    my_keys = pl.ds(pl.multiple_of(c * rows, rows), rows)
    kbuf[my_keys, 0:LAT] = kl[...]
    kr = tn(krt[...], identity(ROPE)).astype(bf16)
    kbuf[my_keys, LAT:KW] = jnp.concatenate([kr, jnp.zeros((rows, KW - LAT - ROPE), bf16)], axis=1)
    zm[t] = lanes_of(idt[...].astype(f32), 0) + lanes_of(sct[...], K)
    zg[t] = g[...]
    for h in range(H):
        obuf[pl.ds(pl.multiple_of(c * OC, OC), OC), h * VD : (h + 1) * VD] = ost[h]
    vbuf[:, pl.ds(pl.multiple_of(c * LR, LR), LR), :] = vs[...]
    pl.semaphore_wait(bar, C + T - 1)


    def v_part(owner, half):
        return vbuf.at[pl.ds(half * Hh, Hh), pl.ds(pl.multiple_of(owner * LR, LR), LR), :]

    def o_part(owner, half):
        return obuf.at[pl.ds(pl.multiple_of(owner * OC + half * OH, OH), OH), :]

    def vo(owner, s, dest):
        return (
            remote(o_part(owner, d), o_part(owner, d), o_ss.at[s], o_rs.at[owner], {"ctx": dest}),
            remote(v_part(owner, d), v_part(owner, d), v_ss.at[s], v_rs.at[owner], {"ctx": dest}),
        )

    def vo_relay(owner, half):
        return (
            remote(o_part(owner, half), o_part(owner, half), so_ss.at[owner], so_rs.at[owner], sib),
            remote(v_part(owner, half), v_part(owner, half), sv_ss.at[owner], sv_rs.at[owner], sib),
        )

    def start(copies):
        for x in copies:
            x.start()

    def wait_recv(copies):
        for x in copies:
            x.wait_recv()

    def wait_send(copies):
        for x in copies:
            x.wait_send()

    for o in range(1, NX):
        start(vo(c, o, at(o, 0)))

    def send_keys(p):
        @pl.when(p > c)
        def _():
            key_copy(c, p).start()

    to_xy(send_keys)
    to_z(lambda p: remote(zm.at[t], zm.at[t], zm_ss.at[p], zm_rs.at[t], {"tp": p}).start())

    def blank(j):
        kbuf[pl.ds(pl.multiple_of(j * rows, rows), rows), :] = jnp.zeros((rows, KW), bf16)

    each(c + 1, C, blank)
    for h in range(H):
        qbuf[h * rows : (h + 1) * rows, 0:LAT] = ql[:, h * LAT : (h + 1) * LAT]
        qbuf[h * rows : (h + 1) * rows, LAT:KW] = jnp.concatenate(
            [qr[:, h * ROPE : (h + 1) * ROPE], jnp.zeros((rows, KW - LAT - ROPE), bf16)], axis=1
        )

    def pass_on(i):
        owner = lax.rem(a + NX - i, NX) * sa + b * sb
        wait_recv(vo(owner, 0, owner))
        for o in range(1, NX):
            start(vo(owner, NX * (i + 1) + o, at(0, o)))
        start(vo_relay(owner, d))

    def key_relay(j):
        key_copy(j, j).wait_recv()
        key_pass(j, side).start()

    each(0, c, key_relay)
    for o in range(1, NX):
        start(vo(c, NX + o, at(0, o)))
    for i in (1, 3, 2) if NX == 4 else range(1, NX):
        pass_on(i)
    each(0, c, lambda j: key_pass(j, 1 - side).wait_recv())
    to_z(lambda p: remote(zg.at[t], zg.at[t], zg_ss.at[p], zg_rs.at[t], {"tp": p}).start())

    S = C * rows
    NB = 4
    SN = S // NB
    MB = 2 * rows

    def sc(n):
        return act.at[n // 2, 0:MB, (n % 2) * SN : (n % 2 + 1) * SN]

    def attend(i):
        r = pl.ds(pl.multiple_of(i * MB, MB), MB)
        q = qbuf[r, :]
        qpos = c * rows + lax.rem(lax.broadcasted_iota(jnp.int32, (MB, SN), 0), rows)
        kpos = lax.broadcasted_iota(jnp.int32, (MB, SN), 1)
        top = jnp.full((MB, 1), -1e30, f32)
        for n in range(NB):
            s = nt(q, kbuf[n * SN : (n + 1) * SN, :]) * scale
            s = jnp.where(kpos + n * SN <= qpos, s, -1e30)
            sc(n)[...] = s
            top = jnp.maximum(top, jnp.max(s, axis=1, keepdims=True))
        total = jnp.zeros((MB, 1), f32)
        acc = jnp.zeros((MB, LAT), f32)
        for n in range(NB):
            p = jnp.exp(sc(n)[...] - top)
            total = total + jnp.sum(p, axis=1, keepdims=True)
            acc = acc + nn(p.astype(bf16), kbuf[n * SN : (n + 1) * SN, 0:LAT])
        qbuf[r, 0:LAT] = (acc / total).astype(bf16)

    each(0, H // 2, attend)

    from_z(lambda p: remote(zm.at[p], zm.at[p], zm_ss.at[p], zm_rs.at[p], {"tp": p}).wait_recv())
    lane = lax.broadcasted_iota(jnp.int32, (NT, NS), 1)
    wanted = (lax.div(lane, SL) * T + t).astype(f32)

    def hit(k):
        return (zm[...].reshape(NT, LANES)[:, k : k + 1] == wanted).astype(f32)

    m = zm[...].reshape(NT, LANES)
    total = m[:, K : K + 1]
    for k in range(1, K):
        total = total + m[:, K + k : K + k + 1]
    match = hit(0)
    weight = match * (route_scale * m[:, K : K + 1] / total)
    for k in range(1, K):
        h_ = hit(k)
        match = match + h_
        weight = weight + h_ * (route_scale * m[:, K + k : K + k + 1] / total)
    below = (
        lax.broadcasted_iota(jnp.int32, (NT, NT), 1) < lax.broadcasted_iota(jnp.int32, (NT, NT), 0)
    ).astype(bf16)
    rank = nn(below, match.astype(bf16))
    pick = jnp.where(rank == lax.rem(lane, SL).astype(f32), match, 0.0)
    place[...] = pick.astype(bf16)
    weight = weight * pick
    w_hi = weight.astype(bf16)
    wts[0] = w_hi
    wts[1] = (weight - w_hi.astype(f32)).astype(bf16)

    from_z(lambda p: remote(zg.at[p], zg.at[p], zg_ss.at[p], zg_rs.at[p], {"tp": p}).wait_recv())

    def g_cols(n):
        return pl.ds(pl.multiple_of(n * CG, CG), CG)

    def place_g(n):
        cols = g_cols(n)
        sx[:, :, cols] = tn(place[...], zg[:, :, cols].reshape(NT, CG)).astype(bf16).reshape(C, SL, CG)
        ag[c, :, cols] = sx[c, :, cols]

    each(0, 2, place_g)

    def relay(bo_):
        def one(ai):
            owner = lax.rem(a + ai, NX) * sa + lax.rem(b + NX - bo_, NX) * sb
            wait_recv(vo(owner, 0, owner))
            start(vo_relay(owner, d))

        each(0, NX, one)

    for o in (1, 3, 2) if NX == 4 else range(1, NX):
        relay(o)

    def xg(n, p, q):
        cols = g_cols(n)
        return remote(sx.at[p, :, cols], ag.at[q, :, cols], xg_ss.at[n, p], xg_rs.at[n, q], {"ctx": p})

    each(0, 2, lambda n: to_xy(lambda p: xg(n, p, c).start()))

    from_xy(lambda p: wait_recv(vo_relay(p, 1 - d)))
    swap_d.start()
    swap_u.start()

    for h in range(H):
        heads[:, h * VD : (h + 1) * VD] = nn(qbuf[h * rows : (h + 1) * rows, 0:LAT], vbuf[h]).astype(bf16)

    def u_cols(n):
        return pl.ds(pl.multiple_of(n * CD, CD), CD)

    def partial(n, p, q):
        cols = u_cols(n)
        return remote(part.at[p, :, cols], rsb.at[q, :, cols], r_ss.at[n, p], r_rs.at[n, q], {"tp": p})

    def project(n):
        cols = u_cols(n)
        part[:, :, cols] = nt(heads[...], obuf[cols, :]).astype(bf16).reshape(T, tok, CD)
        to_z(lambda p: partial(n, p, t).start())
        rsb[t, :, cols] = part[t, :, cols]

    each(0, ND, project)

    def sent_vo(off):
        for o in range(1, NX):
            wait_send(vo(c, NX * off + o, c))

    each(0, NX + 1, sent_vo)
    from_xy(lambda p: wait_send(vo_relay(p, d)))
    pl.semaphore_signal(ready, inc=1, device_id=sib, device_id_type=MESH)
    own_g.start()

    each(0, ND, lambda n: from_z(lambda p: partial(n, p, p).wait_recv()))
    hs = rsb[0].astype(f32)
    for i in range(1, T):
        hs = hs + rsb[i].astype(f32)
    hs = hs + res[...].astype(f32)
    hs_o[...] = hs
    inv = lax.rsqrt(jnp.mean(hs * hs, axis=1, keepdims=True) + norm_eps)
    zu[t] = (hs * inv * row_of(gain)).astype(bf16)

    def z_u(n, p, q):
        cols = u_cols(n)
        return remote(zu.at[q, :, cols], zu.at[q, :, cols], zu_ss.at[n, p], zu_rs.at[n, q], {"tp": p})

    each(0, ND, lambda n: to_z(lambda p: z_u(n, p, t).start()))
    pl.semaphore_wait(ready, 1)
    swap_g.start()
    each(0, 2, lambda n: from_xy(lambda p: xg(n, p, c).wait_send()))

    def x_u(n, p, q):
        cols = u_cols(n)
        return remote(sx.at[p, :, cols], au.at[q, :, cols], xu_ss.at[n, p], xu_rs.at[n, q], {"ctx": p})

    def send_u(n):
        cols = u_cols(n)
        from_z(lambda p: z_u(n, p, p).wait_recv())
        sx[:, :, cols] = tn(place[...], zu[:, :, cols].reshape(NT, CD)).astype(bf16).reshape(C, SL, CD)
        to_xy(lambda p: x_u(n, p, c).start())
        au[c, :, cols] = sx[c, :, cols]

    each(0, ND, send_u)

    own_d.wait()
    swap_d.wait()
    act[2] = jnp.zeros((NS, HID), f32)

    def d_hidden(n):
        from_xy(lambda p: xg(n, p, p).wait_recv())
        cols = g_cols(n)
        act[2] += nt(ag[:, :, cols].reshape(NS, CG), ds_[:, cols])

    each(0, 2, d_hidden)
    own_u.wait()
    swap_u.wait()
    own_g.wait()
    swap_g.wait()
    act[0] = jnp.zeros((NS, HID), f32)
    act[1] = jnp.zeros((NS, HID), f32)

    def gate_up(n):
        from_xy(lambda p: x_u(n, p, p).wait_recv())
        cols = u_cols(n)
        x = au[:, :, cols].reshape(NS, CD)
        act[0] += nn(x, gs[cols, :])
        act[1] += nn(x, us[cols, :])

    each(0, ND, gate_up)

    EB = NS // 4

    def pointwise(i):
        r = pl.ds(pl.multiple_of(i * EB, EB), EB)
        a_, b_, dh = act[0, r, :], act[1, r, :], act[2, r, :]
        sig = jax.nn.sigmoid(a_)
        gated = a_ * sig
        ab[0, r, :] = (gated * b_).astype(bf16)
        ab[1, r, :] = (dh * b_ * (sig * (1.0 + a_ * (1.0 - sig)))).astype(bf16)
        ab[2, r, :] = (dh * gated).astype(bf16)

    each(0, 4, pointwise)

    backs = ((ro, bo), (rd, bd))

    def r_cols(n):
        return pl.ds(pl.multiple_of(n * CR, CR), CR)

    def back(i, n, p, q):
        s_, r_ = backs[i]
        cols = r_cols(n)
        return remote(s_.at[p, :, cols], r_.at[q, :, cols], b_ss.at[i * NR + n, p], b_rs.at[i * NR + n, q], {"ctx": p})

    def w_back(p, q):
        return remote(rw.at[p], bw.at[q], bw_ss.at[p], bw_rs.at[q], {"ctx": p})

    def result(n, wg):
        cols = r_cols(n)
        y = nn(ab[0], ds_[:, cols]).astype(bf16)
        ro[:, :, cols] = y.reshape(C, SL, CR)
        to_xy(lambda p: back(0, n, p, c).start())
        bo[c, :, cols] = ro[c, :, cols]
        return wg + jnp.sum(y.astype(f32) * ag[:, :, cols].reshape(NS, CR).astype(f32), axis=1, keepdims=True)

    wg = lax.fori_loop(0, NR, result, jnp.zeros((NS, 1), f32))
    rw[...] = jnp.broadcast_to(wg, (NS, LANES)).reshape(rw.shape)
    to_xy(lambda p: w_back(p, c).start())
    bw[c] = rw[c]

    def grads(n):
        cols = r_cols(n)
        y = nt(ab[1], gs[cols, :]) + nt(ab[2], us[cols, :])
        rd[:, :, cols] = y.astype(bf16).reshape(C, SL, CR)
        to_xy(lambda p: back(1, n, p, c).start())
        bd[c, :, cols] = rd[c, :, cols]

    each(0, NR, grads)

    each(0, ND, lambda n: to_z(lambda p: partial(n, p, t).wait_send()))
    sums = ((part, fo), (pd, fd))

    def z_back(i, n, p, q):
        s_, r_ = sums[i]
        cols = r_cols(n)
        return remote(s_.at[p, :, cols], r_.at[q, :, cols], y_ss.at[i * NR + n, p], y_rs.at[i * NR + n, q], {"tp": p})

    def w_sum(p, q):
        return remote(pw.at[p], fw.at[q], yw_ss.at[p], yw_rs.at[q], {"tp": p})

    def combine(i):
        def chunk(n):
            cols = r_cols(n)
            from_xy(lambda p: back(i, n, p, p).wait_recv())
            x = backs[i][1][:, :, cols].reshape(NS, CR)
            sums[i][0][:, :, cols] = (nn(wts[0], x) + nn(wts[1], x)).astype(bf16).reshape(T, tok, CR)
            to_z(lambda p: z_back(i, n, p, t).start())
            sums[i][1][t, :, cols] = sums[i][0][t, :, cols]

        each(0, NR, chunk)

    combine(0)
    from_xy(lambda p: w_back(p, p).wait_recv())
    wcol = bw[...].reshape(NS, LANES)
    wlane = lax.broadcasted_iota(jnp.int32, (NT, LANES), 1)
    wgk = jnp.zeros((NT, LANES), f32)
    chosen = place[...].astype(f32)
    for k in range(K):
        v = lax.dot_general(
            hit(k) * chosen, wcol, (((1,), (0,)), ((), ())), preferred_element_type=f32, precision=lax.Precision.HIGHEST
        )
        wgk = jnp.where(wlane == k, v, wgk)
    pw[...] = wgk.reshape(pw.shape)
    to_z(lambda p: w_sum(p, t).start())
    fw[t] = pw[t]
    combine(1)

    def total_of(ref):
        v = ref[0].astype(f32)
        for i in range(1, T):
            v = v + ref[i].astype(f32)
        return v

    each(0, NR, lambda n: from_z(lambda p: z_back(0, n, p, p).wait_recv()))
    so_o[...] = total_of(fo)
    from_z(lambda p: w_sum(p, p).wait_recv())
    wg_o[...] = total_of(fw)

    to_z(lambda p: remote(zm.at[t], zm.at[t], zm_ss.at[p], zm_rs.at[t], {"tp": p}).wait_send())
    to_z(lambda p: remote(zg.at[t], zg.at[t], zg_ss.at[p], zg_rs.at[t], {"tp": p}).wait_send())
    each(0, ND, lambda n: to_z(lambda p: z_u(n, p, t).wait_send()))
    each(0, ND, lambda n: from_xy(lambda p: x_u(n, p, c).wait_send()))
    for i in range(2):
        each(0, NR, lambda n: from_xy(lambda p: back(i, n, p, c).wait_send()))
    from_xy(lambda p: w_back(p, c).wait_send())
    each(c + 1, C, lambda j: key_copy(c, j).wait_send())
    each(0, c, lambda j: key_pass(j, side).wait_send())

    each(0, NR, lambda n: from_z(lambda p: z_back(1, n, p, p).wait_recv()))
    dn_o[...] = total_of(fd)
    to_z(lambda p: w_sum(p, t).wait_send())
    for i in range(2):
        each(0, NR, lambda n: to_z(lambda p: z_back(i, n, p, t).wait_send()))


def final_kernel(K, hs, so, dn, wg, g, sct, gain, lo_o, rg_o, sg_o):
    h = hs[...]
    lo_o[...] = (h + so[...]).astype(bf16)
    wgt = exact_nt(unit_rows(K, 0), wg[...])
    sc = sct[...]
    st = jnp.sum(sc, axis=0, keepdims=True)
    sg_o[...] = route_scale / st * (wgt - jnp.sum(wgt * sc, axis=0, keepdims=True) / st)
    dng = dn[...] * row_of(gain)
    inv = lax.rsqrt(jnp.mean(h * h, axis=1, keepdims=True) + norm_eps)
    proj = jnp.mean(dng * h, axis=1, keepdims=True)
    rg_o[...] = (g[...].astype(f32) + inv * dng - h * (inv * inv * inv * proj)).astype(bf16)


VM = pl.BlockSpec(memory_space=pltpu.VMEM)
ANY = pl.BlockSpec(memory_space=pl.ANY)


def per_device(
    C, T,
    query_latent, query_rotary, key_latent, key_rotary, value_up, out_proj, residual, norm_gain,
    gate_proj, up_proj, down_proj, expert_ids, route_score, out_grad,
):
    rows = query_latent.shape[1]
    H, LR, VD = value_up.shape
    LAT, ROPE = key_latent.shape[2], key_rotary.shape[2]
    KW = LAT + LANES
    tok, D = residual.shape[1:]
    K = expert_ids.shape[2]
    HID = gate_proj.shape[2]
    SL = CAP * T
    NS = C * SL
    NT = T * tok
    NX = math.isqrt(C)
    ND, NR = 4, 4
    gain = norm_gain.reshape(D // LANES, LANES)
    id_t = jnp.swapaxes(expert_ids[0], 0, 1)
    score_t = jnp.swapaxes(route_score[0], 0, 1)
    dma = pltpu.SemaphoreType.DMA
    shape = jax.ShapeDtypeStruct
    vmem = pltpu.VMEM
    xy = (C, SL, D)
    zz = (T, tok, D)

    hs, so, dn, wg = pl.pallas_call(
        functools.partial(main_kernel, C, T, K, ND, NR),
        name="layer",
        out_shape=(shape((tok, D), f32), shape((tok, D), f32), shape((tok, D), f32), shape((tok, LANES), f32)),
        in_specs=[VM] * 11 + [ANY] * 3,
        out_specs=(VM,) * 4,
        scratch_shapes=[
            vmem((H * rows, KW), bf16),
            vmem((C * rows, KW), bf16),
            vmem((H, LAT, VD), bf16),
            vmem((D, H * VD), bf16),
            vmem((D, HID), bf16),
            vmem((HID, D), bf16),
            vmem((rows, H * VD), bf16),
            vmem(zz, bf16), vmem(zz, bf16),
            vmem((T, tok, LANES), f32), vmem(zz, bf16), vmem(zz, bf16),
            vmem(xy, bf16), vmem(xy, bf16), vmem(xy, bf16),
            vmem((3, NS, HID), f32),
            vmem((3, NS, HID), bf16),
            vmem((NT, NS), bf16), vmem((2, NT, NS), bf16),
            vmem(xy, bf16), vmem(xy, bf16), vmem((C, SL, LANES), f32),
            vmem(xy, bf16), vmem(xy, bf16), vmem((C, SL, LANES), f32),
            vmem(zz, bf16), vmem((T, tok, LANES), f32),
            vmem(zz, bf16), vmem(zz, bf16), vmem((T, tok, LANES), f32),
            dma((3,)), dma((3,)), dma((3,)),
            dma((C,)), dma((C,)), dma((C,)), dma((C,)),
            dma((NX * (NX + 1),)), dma((C,)), dma((NX * (NX + 1),)), dma((C,)),
            dma((C,)), dma((C,)), dma((C,)), dma((C,)),
            dma((ND, T)), dma((ND, T)),
            dma((T,)), dma((T,)), dma((T,)), dma((T,)), dma((ND, T)), dma((ND, T)),
            dma((2, C)), dma((2, C)), dma((ND, C)), dma((ND, C)),
            dma((2 * NR, C)), dma((2 * NR, C)), dma((C,)), dma((C,)),
            dma((2 * NR, T)), dma((2 * NR, T)), dma((T,)), dma((T,)),
            pltpu.SemaphoreType.REGULAR,
        ],
        compiler_params=pltpu.CompilerParams(
            collective_id=0, has_side_effects=True, vmem_limit_bytes=60 * 1024 * 1024
        ),
    )(
        query_latent[0], query_rotary[0], key_latent[0], jnp.swapaxes(key_rotary[0], 0, 1), value_up,
        jnp.swapaxes(out_proj, 1, 2), residual[0], gain, out_grad[0], id_t, score_t, gate_proj[0], up_proj[0],
        down_proj[0],
    )
    layer_out, resid_grad, score_grad = pl.pallas_call(
        functools.partial(final_kernel, K),
        name="finish",
        out_shape=(shape((tok, D), bf16), shape((tok, D), bf16), shape((K, tok), f32)),
        in_specs=[VM] * 7,
        out_specs=(VM,) * 3,
    )(hs, so, dn, wg, out_grad[0], score_t, gain)
    return (layer_out[None], resid_grad[None], jnp.swapaxes(score_grad, 0, 1)[None])


def solution(mesh):
    return jax.shard_map(
        functools.partial(per_device, mesh.shape["ctx"], mesh.shape["tp"]),
        mesh=mesh,
        in_specs=(
            P("dp", "ctx", "tp"),
            P("dp", "ctx", "tp"),
            P("dp", "ctx", None),
            P("dp", "ctx", None),
            P("tp", "ctx", None),
            P("tp", None, "ctx"),
            P("dp", ("ctx", "tp"), None),
            P(),
            P(("ctx", "tp"), "dp", None),
            P(("ctx", "tp"), "dp", None),
            P(("ctx", "tp"), "dp", None),
            P("dp", ("ctx", "tp"), None),
            P("dp", ("ctx", "tp"), None),
            P("dp", ("ctx", "tp"), None),
        ),
        out_specs=(
            P("dp", ("ctx", "tp"), None),
            P("dp", ("ctx", "tp"), None),
            P("dp", ("ctx", "tp"), None),
        ),
        check_vma=False,
    )
```

```python
import functools
import math

import jax
import jax.numpy as jnp
from jax import lax
from jax.experimental import pallas as pl
from jax.experimental.pallas import tpu as pltpu
from jax.sharding import PartitionSpec as P

MESH = pl.DeviceIdType.MESH
f32 = jnp.float32
bf16 = jnp.bfloat16
route_scale = 2.5
norm_eps = 1e-06
CAP = 2
LANES = 128


def remote(src, dst, send_sem, recv_sem, device):
    return pltpu.make_async_remote_copy(
        src_ref=src, dst_ref=dst, send_sem=send_sem, recv_sem=recv_sem, device_id=device, device_id_type=MESH
    )


def each(lo, hi, fn):
    def body(i, carry):
        fn(i)
        return carry

    lax.fori_loop(lo, hi, body, 0)


def nt(a, b):
    return lax.dot_general(a, b, (((1,), (1,)), ((), ())), preferred_element_type=f32)


def nn(a, b):
    return lax.dot_general(a, b, (((1,), (0,)), ((), ())), preferred_element_type=f32)


def tn(a, b):
    return lax.dot_general(a, b, (((0,), (0,)), ((), ())), preferred_element_type=f32)


def identity(n):
    return (lax.broadcasted_iota(jnp.int32, (n, n), 0) == lax.broadcasted_iota(jnp.int32, (n, n), 1)).astype(bf16)


def row_of(ref):
    return jnp.concatenate([ref[i : i + 1, :] for i in range(ref.shape[0])], axis=1)


def exact_tn(x, y):
    return lax.dot_general(
        x, y, (((0,), (0,)), ((), ())), preferred_element_type=f32, precision=lax.Precision.HIGHEST
    )


def exact_nt(x, y):
    return lax.dot_general(
        x, y, (((1,), (1,)), ((), ())), preferred_element_type=f32, precision=lax.Precision.HIGHEST
    )


def unit_rows(n, first):
    at_row = lax.broadcasted_iota(jnp.int32, (n, LANES), 0) + first
    return (lax.broadcasted_iota(jnp.int32, (n, LANES), 1) == at_row).astype(f32)


def lanes_of(x, first):
    return exact_tn(x, unit_rows(x.shape[0], first))


def tour(n):
    if n == 4:
        return [(1, 0), (0, 1), (3, 0), (0, 3), (1, 1), (3, 3), (1, 3), (3, 1), (2, 0), (0, 2), (2, 1), (1, 2),
                (2, 3), (3, 2), (2, 2)]
    return [(i % n, i // n) for i in range(1, n * n)]


def main_kernel(
    C, T, K, ND, NR,
    ql, qr, kl, krt, vs, ost, res, gain, g, idt, sct, gw, uw, dw,
    hs_o, so_o, dn_o, wg_o,
    qbuf, kbuf, vbuf, obuf, us, ds_, heads, part, rsb, zm, zg, zu, sx, ag, au, act, ab, place, wts,
    ro, rd, rw, bo, bd, bw, pd, pw, fo, fd, fw,
    wl, w_ss, w_rs, k_ss, k_rs, v_ss, v_rs, o_ss, o_rs, sv_ss, sv_rs, so_ss, so_rs, r_ss, r_rs,
    zm_ss, zm_rs, zg_ss, zg_rs, zu_ss, zu_rs, xg_ss, xg_rs, xu_ss, xu_rs, b_ss, b_rs, bw_ss, bw_rs,
    y_ss, y_rs, yw_ss, yw_rs, ready,
):
    c, t, d = lax.axis_index("ctx"), lax.axis_index("tp"), lax.axis_index("dp")
    NX = math.isqrt(C)
    rows = ql.shape[0]
    H, LR, VD = vs.shape
    LAT = kl.shape[1]
    ROPE = krt.shape[0]
    KW = kbuf.shape[1]
    OC = ost.shape[1]
    OH = OC // 2
    Hh = H // 2
    tok, D = res.shape
    DH, HH = gw.shape[0], dw.shape[0]
    HID = 2 * HH
    SL = CAP * T
    NT = T * tok
    NS = C * SL
    CD, CG, CR = D // ND, D // 2, D // NR
    scale = (VD + ROPE) ** (-0.5)
    sib = {"dp": 1 - d}
    gs = obuf

    row, col = lax.div(c, NX), lax.rem(c, NX)
    a = col * (1 - d) + row * d
    b = row * (1 - d) + col * d
    sa, sb = 1 + (NX - 1) * d, NX - (NX - 1) * d

    def at(da, db):
        return lax.rem(a + da, NX) * sa + lax.rem(b + db, NX) * sb

    hops = tour(NX)

    def to_xy(fn):
        for da, db in hops:
            fn(at(da, db))

    def from_xy(fn):
        each(1, C, lambda off: fn(lax.rem(c + C - off, C)))

    def to_z(fn):
        each(1, T, lambda off: fn(lax.rem(t + off, T)))

    def from_z(fn):
        each(1, T, lambda off: fn(lax.rem(t + T - off, T)))

    bar = pltpu.get_barrier_semaphore()
    from_xy(lambda p: pl.semaphore_signal(bar, inc=1, device_id={"ctx": p}, device_id_type=MESH))
    to_z(lambda p: pl.semaphore_signal(bar, inc=1, device_id={"tp": p}, device_id_type=MESH))
    pl.semaphore_signal(bar, inc=1, device_id=sib, device_id_type=MESH)

    def half_rows(ref, who, n):
        return ref.at[pl.ds(pl.multiple_of(who * n, n), n)]

    own_d = pltpu.make_async_copy(dw, half_rows(ds_, d, HH), wl.at[0])
    own_u = pltpu.make_async_copy(uw, half_rows(us, d, DH), wl.at[1])
    own_g = pltpu.make_async_copy(gw, half_rows(gs, d, DH), wl.at[2])
    own_d.start()
    own_u.start()
    swap_d = remote(dw, half_rows(ds_, d, HH), w_ss.at[0], w_rs.at[0], sib)
    swap_u = remote(uw, half_rows(us, d, DH), w_ss.at[1], w_rs.at[1], sib)
    swap_g = remote(gw, half_rows(gs, d, DH), w_ss.at[2], w_rs.at[2], sib)

    def key_copy(owner, i, p):
        ref = kbuf.at[pl.ds(pl.multiple_of(owner * rows, rows), rows)]
        return remote(ref, ref, k_ss.at[i], k_rs.at[owner], {"ctx": p})

    def y_of(pa, pb):
        return pb * (1 - d) + pa * d

    def first_hops(fn):
        for o in range(1, NX):
            @pl.when(row <= y_of(lax.rem(a + o, NX), b))
            def _():
                fn(key_copy(c, o, at(o, 0)))

    def second_hops(i, fn):
        oa = lax.rem(a + NX - i, NX)
        for o in range(1, NX):
            @pl.when(y_of(oa, b) <= y_of(a, lax.rem(b + o, NX)))
            def _():
                fn(key_copy(oa * sa + b * sb, NX * (i + 1) + o, at(0, o)))

    def key_in(oa, ob):
        owner = oa * sa + ob * sb

        @pl.when(y_of(oa, ob) <= row)
        def _():
            key_copy(owner, 0, owner).wait_recv()

    my_keys = pl.ds(pl.multiple_of(c * rows, rows), rows)
    kbuf[my_keys, 0:LAT] = kl[...]
    kr = tn(krt[...], identity(ROPE)).astype(bf16)
    kbuf[my_keys, LAT:KW] = jnp.concatenate([kr, jnp.zeros((rows, KW - LAT - ROPE), bf16)], axis=1)
    zm[t] = lanes_of(idt[...].astype(f32), 0) + lanes_of(sct[...], K)
    zg[t] = g[...]
    for h in range(H):
        obuf[pl.ds(pl.multiple_of(c * OC, OC), OC), h * VD : (h + 1) * VD] = ost[h]
    vbuf[:, pl.ds(pl.multiple_of(c * LR, LR), LR), :] = vs[...]
    pl.semaphore_wait(bar, C + T - 1)


    def v_part(owner, half):
        return vbuf.at[pl.ds(half * Hh, Hh), pl.ds(pl.multiple_of(owner * LR, LR), LR), :]

    def o_part(owner, half):
        return obuf.at[pl.ds(pl.multiple_of(owner * OC + half * OH, OH), OH), :]

    def vo(owner, s, dest):
        return (
            remote(o_part(owner, d), o_part(owner, d), o_ss.at[s], o_rs.at[owner], {"ctx": dest}),
            remote(v_part(owner, d), v_part(owner, d), v_ss.at[s], v_rs.at[owner], {"ctx": dest}),
        )

    def vo_relay(owner, half):
        return (
            remote(o_part(owner, half), o_part(owner, half), so_ss.at[owner], so_rs.at[owner], sib),
            remote(v_part(owner, half), v_part(owner, half), sv_ss.at[owner], sv_rs.at[owner], sib),
        )

    def start(copies):
        for x in copies:
            x.start()

    def wait_recv(copies):
        for x in copies:
            x.wait_recv()

    def wait_send(copies):
        for x in copies:
            x.wait_send()

    for o in range(1, NX):
        start(vo(c, o, at(o, 0)))

    first_hops(lambda x: x.start())
    second_hops(0, lambda x: x.start())
    to_z(lambda p: remote(zm.at[t], zm.at[t], zm_ss.at[p], zm_rs.at[t], {"tp": p}).start())
    to_z(lambda p: remote(zg.at[t], zg.at[t], zg_ss.at[p], zg_rs.at[t], {"tp": p}).start())

    def blank(j):
        kbuf[pl.ds(pl.multiple_of(j * rows, rows), rows), :] = jnp.zeros((rows, KW), bf16)

    each((row + 1) * NX, C, blank)
    for h in range(H):
        qbuf[h * rows : (h + 1) * rows, 0:LAT] = ql[:, h * LAT : (h + 1) * LAT]
        qbuf[h * rows : (h + 1) * rows, LAT:KW] = jnp.concatenate(
            [qr[:, h * ROPE : (h + 1) * ROPE], jnp.zeros((rows, KW - LAT - ROPE), bf16)], axis=1
        )

    def pass_on(i):
        owner = lax.rem(a + NX - i, NX) * sa + b * sb
        wait_recv(vo(owner, 0, owner))
        for o in range(1, NX):
            start(vo(owner, NX * (i + 1) + o, at(0, o)))
        start(vo_relay(owner, d))

    for i in (1, 3, 2) if NX == 4 else range(1, NX):
        key_in(lax.rem(a + NX - i, NX), b)
        second_hops(i, lambda x: x.start())
    for o in range(1, NX):
        start(vo(c, NX + o, at(0, o)))
    for i in (1, 3, 2) if NX == 4 else range(1, NX):
        pass_on(i)
    for o in range(1, NX):
        each(0, NX, lambda oa: key_in(oa, lax.rem(b + o, NX)))

    S = C * rows
    NB = 4
    SN = S // NB
    MB = 2 * rows

    def sc(n):
        return act.at[n // 2, 0:MB, (n % 2) * SN : (n % 2 + 1) * SN]

    def attend(i):
        r = pl.ds(pl.multiple_of(i * MB, MB), MB)
        q = qbuf[r, :]
        qpos = c * rows + lax.rem(lax.broadcasted_iota(jnp.int32, (MB, SN), 0), rows)
        kpos = lax.broadcasted_iota(jnp.int32, (MB, SN), 1)
        top = jnp.full((MB, 1), -1e30, f32)
        for n in range(NB):
            s = nt(q, kbuf[n * SN : (n + 1) * SN, :]) * scale
            s = jnp.where(kpos + n * SN <= qpos, s, -1e30)
            sc(n)[...] = s
            top = jnp.maximum(top, jnp.max(s, axis=1, keepdims=True))
        total = jnp.zeros((MB, 1), f32)
        acc = jnp.zeros((MB, LAT), f32)
        for n in range(NB):
            p = jnp.exp(sc(n)[...] - top)
            total = total + jnp.sum(p, axis=1, keepdims=True)
            acc = acc + nn(p.astype(bf16), kbuf[n * SN : (n + 1) * SN, 0:LAT])
        qbuf[r, 0:LAT] = (acc / total).astype(bf16)

    each(0, H // 2, attend)

    from_z(lambda p: remote(zm.at[p], zm.at[p], zm_ss.at[p], zm_rs.at[p], {"tp": p}).wait_recv())
    lane = lax.broadcasted_iota(jnp.int32, (NT, NS), 1)
    wanted = (lax.div(lane, SL) * T + t).astype(f32)

    def hit(k):
        return (zm[...].reshape(NT, LANES)[:, k : k + 1] == wanted).astype(f32)

    m = zm[...].reshape(NT, LANES)
    total = m[:, K : K + 1]
    for k in range(1, K):
        total = total + m[:, K + k : K + k + 1]
    match = hit(0)
    weight = match * (route_scale * m[:, K : K + 1] / total)
    for k in range(1, K):
        h_ = hit(k)
        match = match + h_
        weight = weight + h_ * (route_scale * m[:, K + k : K + k + 1] / total)
    below = (
        lax.broadcasted_iota(jnp.int32, (NT, NT), 1) < lax.broadcasted_iota(jnp.int32, (NT, NT), 0)
    ).astype(bf16)
    rank = nn(below, match.astype(bf16))
    pick = jnp.where(rank == lax.rem(lane, SL).astype(f32), match, 0.0)
    place[...] = pick.astype(bf16)
    weight = weight * pick
    w_hi = weight.astype(bf16)
    wts[0] = w_hi
    wts[1] = (weight - w_hi.astype(f32)).astype(bf16)

    from_z(lambda p: remote(zg.at[p], zg.at[p], zg_ss.at[p], zg_rs.at[p], {"tp": p}).wait_recv())

    def g_cols(n):
        return pl.ds(pl.multiple_of(n * CG, CG), CG)

    def place_g(n):
        cols = g_cols(n)
        sx[:, :, cols] = tn(place[...], zg[:, :, cols].reshape(NT, CG)).astype(bf16).reshape(C, SL, CG)
        ag[c, :, cols] = sx[c, :, cols]

    each(0, 2, place_g)

    def relay(bo_):
        def one(ai):
            owner = lax.rem(a + ai, NX) * sa + lax.rem(b + NX - bo_, NX) * sb
            wait_recv(vo(owner, 0, owner))
            start(vo_relay(owner, d))

        each(0, NX, one)

    for o in (1, 3, 2) if NX == 4 else range(1, NX):
        relay(o)

    def xg(n, p, q):
        cols = g_cols(n)
        return remote(sx.at[p, :, cols], ag.at[q, :, cols], xg_ss.at[n, p], xg_rs.at[n, q], {"ctx": p})

    each(0, 2, lambda n: to_xy(lambda p: xg(n, p, c).start()))

    from_xy(lambda p: wait_recv(vo_relay(p, 1 - d)))
    swap_d.start()
    swap_u.start()

    for h in range(H):
        heads[:, h * VD : (h + 1) * VD] = nn(qbuf[h * rows : (h + 1) * rows, 0:LAT], vbuf[h]).astype(bf16)

    def u_cols(n):
        return pl.ds(pl.multiple_of(n * CD, CD), CD)

    def partial(n, p, q):
        cols = u_cols(n)
        return remote(part.at[p, :, cols], rsb.at[q, :, cols], r_ss.at[n, p], r_rs.at[n, q], {"tp": p})

    def project(n):
        cols = u_cols(n)
        part[:, :, cols] = nt(heads[...], obuf[cols, :]).astype(bf16).reshape(T, tok, CD)
        to_z(lambda p: partial(n, p, t).start())
        rsb[t, :, cols] = part[t, :, cols]

    each(0, ND, project)

    def sent_vo(off):
        for o in range(1, NX):
            wait_send(vo(c, NX * off + o, c))

    each(0, NX + 1, sent_vo)
    from_xy(lambda p: wait_send(vo_relay(p, d)))
    pl.semaphore_signal(ready, inc=1, device_id=sib, device_id_type=MESH)
    own_g.start()

    each(0, ND, lambda n: from_z(lambda p: partial(n, p, p).wait_recv()))
    hs = rsb[0].astype(f32)
    for i in range(1, T):
        hs = hs + rsb[i].astype(f32)
    hs = hs + res[...].astype(f32)
    hs_o[...] = hs
    inv = lax.rsqrt(jnp.mean(hs * hs, axis=1, keepdims=True) + norm_eps)
    zu[t] = (hs * inv * row_of(gain)).astype(bf16)

    def z_u(n, p, q):
        cols = u_cols(n)
        return remote(zu.at[q, :, cols], zu.at[q, :, cols], zu_ss.at[n, p], zu_rs.at[n, q], {"tp": p})

    each(0, ND, lambda n: to_z(lambda p: z_u(n, p, t).start()))
    pl.semaphore_wait(ready, 1)
    swap_g.start()
    each(0, 2, lambda n: from_xy(lambda p: xg(n, p, c).wait_send()))

    def x_u(n, p, q):
        cols = u_cols(n)
        return remote(sx.at[p, :, cols], au.at[q, :, cols], xu_ss.at[n, p], xu_rs.at[n, q], {"ctx": p})

    def send_u(n):
        cols = u_cols(n)
        from_z(lambda p: z_u(n, p, p).wait_recv())
        sx[:, :, cols] = tn(place[...], zu[:, :, cols].reshape(NT, CD)).astype(bf16).reshape(C, SL, CD)
        to_xy(lambda p: x_u(n, p, c).start())
        au[c, :, cols] = sx[c, :, cols]

    each(0, ND, send_u)

    own_d.wait()
    swap_d.wait()
    act[2] = jnp.zeros((NS, HID), f32)

    def d_hidden(n):
        from_xy(lambda p: xg(n, p, p).wait_recv())
        cols = g_cols(n)
        act[2] += nt(ag[:, :, cols].reshape(NS, CG), ds_[:, cols])

    each(0, 2, d_hidden)
    own_u.wait()
    swap_u.wait()
    own_g.wait()
    swap_g.wait()
    act[0] = jnp.zeros((NS, HID), f32)
    act[1] = jnp.zeros((NS, HID), f32)

    def gate_up(n):
        from_xy(lambda p: x_u(n, p, p).wait_recv())
        cols = u_cols(n)
        x = au[:, :, cols].reshape(NS, CD)
        act[0] += nn(x, gs[cols, :])
        act[1] += nn(x, us[cols, :])

    each(0, ND, gate_up)

    EB = NS // 4

    def pointwise(i):
        r = pl.ds(pl.multiple_of(i * EB, EB), EB)
        a_, b_, dh = act[0, r, :], act[1, r, :], act[2, r, :]
        sig = jax.nn.sigmoid(a_)
        gated = a_ * sig
        ab[0, r, :] = (gated * b_).astype(bf16)
        ab[1, r, :] = (dh * b_ * (sig * (1.0 + a_ * (1.0 - sig)))).astype(bf16)
        ab[2, r, :] = (dh * gated).astype(bf16)

    each(0, 4, pointwise)

    backs = ((ro, bo), (rd, bd))

    def r_cols(n):
        return pl.ds(pl.multiple_of(n * CR, CR), CR)

    def back(i, n, p, q):
        s_, r_ = backs[i]
        cols = r_cols(n)
        return remote(s_.at[p, :, cols], r_.at[q, :, cols], b_ss.at[i * NR + n, p], b_rs.at[i * NR + n, q], {"ctx": p})

    def w_back(p, q):
        return remote(rw.at[p], bw.at[q], bw_ss.at[p], bw_rs.at[q], {"ctx": p})

    def result(n, wg):
        cols = r_cols(n)
        y = nn(ab[0], ds_[:, cols]).astype(bf16)
        ro[:, :, cols] = y.reshape(C, SL, CR)
        to_xy(lambda p: back(0, n, p, c).start())
        bo[c, :, cols] = ro[c, :, cols]
        return wg + jnp.sum(y.astype(f32) * ag[:, :, cols].reshape(NS, CR).astype(f32), axis=1, keepdims=True)

    wg = lax.fori_loop(0, NR, result, jnp.zeros((NS, 1), f32))
    rw[...] = jnp.broadcast_to(wg, (NS, LANES)).reshape(rw.shape)
    to_xy(lambda p: w_back(p, c).start())
    bw[c] = rw[c]

    def grads(n):
        cols = r_cols(n)
        y = nt(ab[1], gs[cols, :]) + nt(ab[2], us[cols, :])
        rd[:, :, cols] = y.astype(bf16).reshape(C, SL, CR)
        to_xy(lambda p: back(1, n, p, c).start())
        bd[c, :, cols] = rd[c, :, cols]

    each(0, NR, grads)

    each(0, ND, lambda n: to_z(lambda p: partial(n, p, t).wait_send()))
    sums = ((part, fo), (pd, fd))

    def z_back(i, n, p, q):
        s_, r_ = sums[i]
        cols = r_cols(n)
        return remote(s_.at[p, :, cols], r_.at[q, :, cols], y_ss.at[i * NR + n, p], y_rs.at[i * NR + n, q], {"tp": p})

    def w_sum(p, q):
        return remote(pw.at[p], fw.at[q], yw_ss.at[p], yw_rs.at[q], {"tp": p})

    def combine(i):
        def chunk(n):
            cols = r_cols(n)
            from_xy(lambda p: back(i, n, p, p).wait_recv())
            x = backs[i][1][:, :, cols].reshape(NS, CR)
            sums[i][0][:, :, cols] = (nn(wts[0], x) + nn(wts[1], x)).astype(bf16).reshape(T, tok, CR)
            to_z(lambda p: z_back(i, n, p, t).start())
            sums[i][1][t, :, cols] = sums[i][0][t, :, cols]

        each(0, NR, chunk)

    combine(0)
    from_xy(lambda p: w_back(p, p).wait_recv())
    wcol = bw[...].reshape(NS, LANES)
    wlane = lax.broadcasted_iota(jnp.int32, (NT, LANES), 1)
    wgk = jnp.zeros((NT, LANES), f32)
    chosen = place[...].astype(f32)
    for k in range(K):
        v = lax.dot_general(
            hit(k) * chosen, wcol, (((1,), (0,)), ((), ())), preferred_element_type=f32, precision=lax.Precision.HIGHEST
        )
        wgk = jnp.where(wlane == k, v, wgk)
    pw[...] = wgk.reshape(pw.shape)
    to_z(lambda p: w_sum(p, t).start())
    fw[t] = pw[t]
    combine(1)

    def total_of(ref):
        v = ref[0].astype(f32)
        for i in range(1, T):
            v = v + ref[i].astype(f32)
        return v

    each(0, NR, lambda n: from_z(lambda p: z_back(0, n, p, p).wait_recv()))
    so_o[...] = total_of(fo)
    from_z(lambda p: w_sum(p, p).wait_recv())
    wg_o[...] = total_of(fw)

    to_z(lambda p: remote(zm.at[t], zm.at[t], zm_ss.at[p], zm_rs.at[t], {"tp": p}).wait_send())
    to_z(lambda p: remote(zg.at[t], zg.at[t], zg_ss.at[p], zg_rs.at[t], {"tp": p}).wait_send())
    each(0, ND, lambda n: to_z(lambda p: z_u(n, p, t).wait_send()))
    each(0, ND, lambda n: from_xy(lambda p: x_u(n, p, c).wait_send()))
    for i in range(2):
        each(0, NR, lambda n: from_xy(lambda p: back(i, n, p, c).wait_send()))
    from_xy(lambda p: w_back(p, c).wait_send())
    first_hops(lambda x: x.wait_send())
    for i in range(NX):
        second_hops(i, lambda x: x.wait_send())

    each(0, NR, lambda n: from_z(lambda p: z_back(1, n, p, p).wait_recv()))
    dn_o[...] = total_of(fd)
    to_z(lambda p: w_sum(p, t).wait_send())
    for i in range(2):
        each(0, NR, lambda n: to_z(lambda p: z_back(i, n, p, t).wait_send()))


def final_kernel(K, hs, so, dn, wg, g, sct, gain, lo_o, rg_o, sg_o):
    h = hs[...]
    lo_o[...] = (h + so[...]).astype(bf16)
    wgt = exact_nt(unit_rows(K, 0), wg[...])
    sc = sct[...]
    st = jnp.sum(sc, axis=0, keepdims=True)
    sg_o[...] = route_scale / st * (wgt - jnp.sum(wgt * sc, axis=0, keepdims=True) / st)
    dng = dn[...] * row_of(gain)
    inv = lax.rsqrt(jnp.mean(h * h, axis=1, keepdims=True) + norm_eps)
    proj = jnp.mean(dng * h, axis=1, keepdims=True)
    rg_o[...] = (g[...].astype(f32) + inv * dng - h * (inv * inv * inv * proj)).astype(bf16)


VM = pl.BlockSpec(memory_space=pltpu.VMEM)
ANY = pl.BlockSpec(memory_space=pl.ANY)


def per_device(
    C, T,
    query_latent, query_rotary, key_latent, key_rotary, value_up, out_proj, residual, norm_gain,
    gate_proj, up_proj, down_proj, expert_ids, route_score, out_grad,
):
    rows = query_latent.shape[1]
    H, LR, VD = value_up.shape
    LAT, ROPE = key_latent.shape[2], key_rotary.shape[2]
    KW = LAT + LANES
    tok, D = residual.shape[1:]
    K = expert_ids.shape[2]
    HID = gate_proj.shape[2]
    SL = CAP * T
    NS = C * SL
    NT = T * tok
    NX = math.isqrt(C)
    ND, NR = 4, 4
    gain = norm_gain.reshape(D // LANES, LANES)
    id_t = jnp.swapaxes(expert_ids[0], 0, 1)
    score_t = jnp.swapaxes(route_score[0], 0, 1)
    dma = pltpu.SemaphoreType.DMA
    shape = jax.ShapeDtypeStruct
    vmem = pltpu.VMEM
    xy = (C, SL, D)
    zz = (T, tok, D)

    hs, so, dn, wg = pl.pallas_call(
        functools.partial(main_kernel, C, T, K, ND, NR),
        name="layer",
        out_shape=(shape((tok, D), f32), shape((tok, D), f32), shape((tok, D), f32), shape((tok, LANES), f32)),
        in_specs=[VM] * 11 + [ANY] * 3,
        out_specs=(VM,) * 4,
        scratch_shapes=[
            vmem((H * rows, KW), bf16),
            vmem((C * rows, KW), bf16),
            vmem((H, LAT, VD), bf16),
            vmem((D, H * VD), bf16),
            vmem((D, HID), bf16),
            vmem((HID, D), bf16),
            vmem((rows, H * VD), bf16),
            vmem(zz, bf16), vmem(zz, bf16),
            vmem((T, tok, LANES), f32), vmem(zz, bf16), vmem(zz, bf16),
            vmem(xy, bf16), vmem(xy, bf16), vmem(xy, bf16),
            vmem((3, NS, HID), f32),
            vmem((3, NS, HID), bf16),
            vmem((NT, NS), bf16), vmem((2, NT, NS), bf16),
            vmem(xy, bf16), vmem(xy, bf16), vmem((C, SL, LANES), f32),
            vmem(xy, bf16), vmem(xy, bf16), vmem((C, SL, LANES), f32),
            vmem(zz, bf16), vmem((T, tok, LANES), f32),
            vmem(zz, bf16), vmem(zz, bf16), vmem((T, tok, LANES), f32),
            dma((3,)), dma((3,)), dma((3,)),
            dma((NX * (NX + 1),)), dma((C,)),
            dma((NX * (NX + 1),)), dma((C,)), dma((NX * (NX + 1),)), dma((C,)),
            dma((C,)), dma((C,)), dma((C,)), dma((C,)),
            dma((ND, T)), dma((ND, T)),
            dma((T,)), dma((T,)), dma((T,)), dma((T,)), dma((ND, T)), dma((ND, T)),
            dma((2, C)), dma((2, C)), dma((ND, C)), dma((ND, C)),
            dma((2 * NR, C)), dma((2 * NR, C)), dma((C,)), dma((C,)),
            dma((2 * NR, T)), dma((2 * NR, T)), dma((T,)), dma((T,)),
            pltpu.SemaphoreType.REGULAR,
        ],
        compiler_params=pltpu.CompilerParams(
            collective_id=0, has_side_effects=True, vmem_limit_bytes=60 * 1024 * 1024
        ),
    )(
        query_latent[0], query_rotary[0], key_latent[0], jnp.swapaxes(key_rotary[0], 0, 1), value_up,
        jnp.swapaxes(out_proj, 1, 2), residual[0], gain, out_grad[0], id_t, score_t, gate_proj[0], up_proj[0],
        down_proj[0],
    )
    layer_out, resid_grad, score_grad = pl.pallas_call(
        functools.partial(final_kernel, K),
        name="finish",
        out_shape=(shape((tok, D), bf16), shape((tok, D), bf16), shape((K, tok), f32)),
        in_specs=[VM] * 7,
        out_specs=(VM,) * 3,
    )(hs, so, dn, wg, out_grad[0], score_t, gain)
    return (layer_out[None], resid_grad[None], jnp.swapaxes(score_grad, 0, 1)[None])


def solution(mesh):
    return jax.shard_map(
        functools.partial(per_device, mesh.shape["ctx"], mesh.shape["tp"]),
        mesh=mesh,
        in_specs=(
            P("dp", "ctx", "tp"),
            P("dp", "ctx", "tp"),
            P("dp", "ctx", None),
            P("dp", "ctx", None),
            P("tp", "ctx", None),
            P("tp", None, "ctx"),
            P("dp", ("ctx", "tp"), None),
            P(),
            P(("ctx", "tp"), "dp", None),
            P(("ctx", "tp"), "dp", None),
            P(("ctx", "tp"), "dp", None),
            P("dp", ("ctx", "tp"), None),
            P("dp", ("ctx", "tp"), None),
            P("dp", ("ctx", "tp"), None),
        ),
        out_specs=(
            P("dp", ("ctx", "tp"), None),
            P("dp", ("ctx", "tp"), None),
            P("dp", ("ctx", "tp"), None),
        ),
        check_vma=False,
    )
```

```python
import functools
import math

import jax
import jax.numpy as jnp
from jax import lax
from jax.experimental import pallas as pl
from jax.experimental.pallas import tpu as pltpu
from jax.sharding import PartitionSpec as P

MESH = pl.DeviceIdType.MESH
f32 = jnp.float32
bf16 = jnp.bfloat16
route_scale = 2.5
norm_eps = 1e-06
CAP = 2
LANES = 128


def remote(src, dst, send_sem, recv_sem, device):
    return pltpu.make_async_remote_copy(
        src_ref=src, dst_ref=dst, send_sem=send_sem, recv_sem=recv_sem, device_id=device, device_id_type=MESH
    )


def each(lo, hi, fn):
    def body(i, carry):
        fn(i)
        return carry

    lax.fori_loop(lo, hi, body, 0)


def nt(a, b):
    return lax.dot_general(a, b, (((1,), (1,)), ((), ())), preferred_element_type=f32)


def nn(a, b):
    return lax.dot_general(a, b, (((1,), (0,)), ((), ())), preferred_element_type=f32)


def tn(a, b):
    return lax.dot_general(a, b, (((0,), (0,)), ((), ())), preferred_element_type=f32)


def identity(n):
    return (lax.broadcasted_iota(jnp.int32, (n, n), 0) == lax.broadcasted_iota(jnp.int32, (n, n), 1)).astype(bf16)


def row_of(ref):
    return jnp.concatenate([ref[i : i + 1, :] for i in range(ref.shape[0])], axis=1)


def exact_tn(x, y):
    return lax.dot_general(
        x, y, (((0,), (0,)), ((), ())), preferred_element_type=f32, precision=lax.Precision.HIGHEST
    )


def exact_nt(x, y):
    return lax.dot_general(
        x, y, (((1,), (1,)), ((), ())), preferred_element_type=f32, precision=lax.Precision.HIGHEST
    )


def unit_rows(n, first):
    at_row = lax.broadcasted_iota(jnp.int32, (n, LANES), 0) + first
    return (lax.broadcasted_iota(jnp.int32, (n, LANES), 1) == at_row).astype(f32)


def lanes_of(x, first):
    return exact_tn(x, unit_rows(x.shape[0], first))


def tour(n):
    if n == 4:
        return [(1, 0), (0, 1), (3, 0), (0, 3), (1, 1), (3, 3), (1, 3), (3, 1), (2, 0), (0, 2), (2, 1), (1, 2),
                (2, 3), (3, 2), (2, 2)]
    return [(i % n, i // n) for i in range(1, n * n)]


def main_kernel(
    C, T, K, ND, NR,
    ql, qr, kl, krt, vs, ost, res, gain, g, idt, sct, gw, uw, dw,
    hs_o, so_o, dn_o, wg_o,
    qbuf, kbuf, vbuf, obuf, us, ds_, heads, part, rsb, zm, zg, zu, sx, ag, au, act, ab, place, wts,
    ro, rd, rw, bo, bd, bw, pd, pw, fo, fd, fw,
    wl, w_ss, w_rs, k_ss, k_rs, v_ss, v_rs, o_ss, o_rs, sv_ss, sv_rs, so_ss, so_rs, r_ss, r_rs,
    zm_ss, zm_rs, zg_ss, zg_rs, zu_ss, zu_rs, xg_ss, xg_rs, xu_ss, xu_rs, b_ss, b_rs, bw_ss, bw_rs,
    y_ss, y_rs, yw_ss, yw_rs, ready,
):
    c, t, d = lax.axis_index("ctx"), lax.axis_index("tp"), lax.axis_index("dp")
    NX = math.isqrt(C)
    rows = ql.shape[0]
    H, LR, VD = vs.shape
    LAT = kl.shape[1]
    ROPE = krt.shape[0]
    KW = kbuf.shape[1]
    OC = ost.shape[1]
    OH = OC // 2
    Hh = H // 2
    tok, D = res.shape
    DH, HH = gw.shape[0], dw.shape[0]
    HID = 2 * HH
    SL = CAP * T
    NT = T * tok
    NS = C * SL
    CD, CG, CR = D // ND, D // 2, D // NR
    scale = (VD + ROPE) ** (-0.5)
    sib = {"dp": 1 - d}
    gs = obuf

    row, col = lax.div(c, NX), lax.rem(c, NX)
    a = col * (1 - d) + row * d
    b = row * (1 - d) + col * d
    sa, sb = 1 + (NX - 1) * d, NX - (NX - 1) * d

    def at(da, db):
        return lax.rem(a + da, NX) * sa + lax.rem(b + db, NX) * sb

    hops = tour(NX)

    def to_xy(fn):
        for da, db in hops:
            fn(at(da, db))

    def from_xy(fn):
        each(1, C, lambda off: fn(lax.rem(c + C - off, C)))

    def to_z(fn):
        each(1, T, lambda off: fn(lax.rem(t + off, T)))

    def from_z(fn):
        each(1, T, lambda off: fn(lax.rem(t + T - off, T)))

    bar = pltpu.get_barrier_semaphore()
    from_xy(lambda p: pl.semaphore_signal(bar, inc=1, device_id={"ctx": p}, device_id_type=MESH))
    to_z(lambda p: pl.semaphore_signal(bar, inc=1, device_id={"tp": p}, device_id_type=MESH))
    pl.semaphore_signal(bar, inc=1, device_id=sib, device_id_type=MESH)

    def half_rows(ref, who, n):
        return ref.at[pl.ds(pl.multiple_of(who * n, n), n)]

    own_d = pltpu.make_async_copy(dw, half_rows(ds_, d, HH), wl.at[0])
    own_u = pltpu.make_async_copy(uw, half_rows(us, d, DH), wl.at[1])
    own_g = pltpu.make_async_copy(gw, half_rows(gs, d, DH), wl.at[2])
    own_d.start()
    own_u.start()
    swap_d = remote(dw, half_rows(ds_, d, HH), w_ss.at[0], w_rs.at[0], sib)
    swap_u = remote(uw, half_rows(us, d, DH), w_ss.at[1], w_rs.at[1], sib)
    swap_g = remote(gw, half_rows(gs, d, DH), w_ss.at[2], w_rs.at[2], sib)

    def key_copy(owner, i, p):
        ref = kbuf.at[pl.ds(pl.multiple_of(owner * rows, rows), rows)]
        return remote(ref, ref, k_ss.at[i], k_rs.at[owner], {"ctx": p})

    def y_of(pa, pb):
        return pb * (1 - d) + pa * d

    def first_hops(fn):
        for o in range(1, NX):
            @pl.when(row <= y_of(lax.rem(a + o, NX), b))
            def _():
                fn(key_copy(c, o, at(o, 0)))

    def second_hops(i, fn):
        oa = lax.rem(a + NX - i, NX)
        for o in range(1, NX):
            @pl.when(y_of(oa, b) <= y_of(a, lax.rem(b + o, NX)))
            def _():
                fn(key_copy(oa * sa + b * sb, NX * (i + 1) + o, at(0, o)))

    def key_in(oa, ob):
        owner = oa * sa + ob * sb

        @pl.when(y_of(oa, ob) <= row)
        def _():
            key_copy(owner, 0, owner).wait_recv()

    my_keys = pl.ds(pl.multiple_of(c * rows, rows), rows)
    kbuf[my_keys, 0:LAT] = kl[...]
    kr = tn(krt[...], identity(ROPE)).astype(bf16)
    kbuf[my_keys, LAT:KW] = jnp.concatenate([kr, jnp.zeros((rows, KW - LAT - ROPE), bf16)], axis=1)
    zm[t] = lanes_of(idt[...].astype(f32), 0) + lanes_of(sct[...], K)
    zg[t] = g[...]
    for h in range(H):
        obuf[pl.ds(pl.multiple_of(c * OC, OC), OC), h * VD : (h + 1) * VD] = ost[h]
    vbuf[:, pl.ds(pl.multiple_of(c * LR, LR), LR), :] = vs[...]
    pl.semaphore_wait(bar, C + T - 1)


    def v_part(owner, half):
        return vbuf.at[pl.ds(half * Hh, Hh), pl.ds(pl.multiple_of(owner * LR, LR), LR), :]

    def o_part(owner, half):
        return obuf.at[pl.ds(pl.multiple_of(owner * OC + half * OH, OH), OH), :]

    def vo(owner, s, dest):
        return (
            remote(o_part(owner, d), o_part(owner, d), o_ss.at[s], o_rs.at[owner], {"ctx": dest}),
            remote(v_part(owner, d), v_part(owner, d), v_ss.at[s], v_rs.at[owner], {"ctx": dest}),
        )

    def vo_relay(owner, half):
        return (
            remote(o_part(owner, half), o_part(owner, half), so_ss.at[owner], so_rs.at[owner], sib),
            remote(v_part(owner, half), v_part(owner, half), sv_ss.at[owner], sv_rs.at[owner], sib),
        )

    def start(copies):
        for x in copies:
            x.start()

    def wait_recv(copies):
        for x in copies:
            x.wait_recv()

    def wait_send(copies):
        for x in copies:
            x.wait_send()

    for o in range(1, NX):
        start(vo(c, o, at(o, 0)))

    first_hops(lambda x: x.start())
    second_hops(0, lambda x: x.start())
    to_z(lambda p: remote(zm.at[t], zm.at[t], zm_ss.at[p], zm_rs.at[t], {"tp": p}).start())
    to_z(lambda p: remote(zg.at[t], zg.at[t], zg_ss.at[p], zg_rs.at[t], {"tp": p}).start())

    def blank(j):
        kbuf[pl.ds(pl.multiple_of(j * rows, rows), rows), :] = jnp.zeros((rows, KW), bf16)

    each((row + 1) * NX, C, blank)
    for h in range(H):
        qbuf[h * rows : (h + 1) * rows, 0:LAT] = ql[:, h * LAT : (h + 1) * LAT]
        qbuf[h * rows : (h + 1) * rows, LAT:KW] = jnp.concatenate(
            [qr[:, h * ROPE : (h + 1) * ROPE], jnp.zeros((rows, KW - LAT - ROPE), bf16)], axis=1
        )

    def pass_on(i):
        owner = lax.rem(a + NX - i, NX) * sa + b * sb
        wait_recv(vo(owner, 0, owner))
        for o in range(1, NX):
            start(vo(owner, NX * (i + 1) + o, at(0, o)))
        start(vo_relay(owner, d))

    for i in (1, 3, 2) if NX == 4 else range(1, NX):
        key_in(lax.rem(a + NX - i, NX), b)
        second_hops(i, lambda x: x.start())
    for o in range(1, NX):
        start(vo(c, NX + o, at(0, o)))
    for i in (1, 3, 2) if NX == 4 else range(1, NX):
        pass_on(i)
    for o in range(1, NX):
        each(0, NX, lambda oa: key_in(oa, lax.rem(b + o, NX)))

    S = C * rows
    NB = 4
    SN = S // NB
    MB = 2 * rows

    def sc(n):
        return act.at[n // 2, 0:MB, (n % 2) * SN : (n % 2 + 1) * SN]

    def attend(i):
        r = pl.ds(pl.multiple_of(i * MB, MB), MB)
        q = qbuf[r, :]
        qpos = c * rows + lax.rem(lax.broadcasted_iota(jnp.int32, (MB, SN), 0), rows)
        kpos = lax.broadcasted_iota(jnp.int32, (MB, SN), 1)
        top = jnp.full((MB, 1), -1e30, f32)
        for n in range(NB):
            s = nt(q, kbuf[n * SN : (n + 1) * SN, :]) * scale
            s = jnp.where(kpos + n * SN <= qpos, s, -1e30)
            sc(n)[...] = s
            top = jnp.maximum(top, jnp.max(s, axis=1, keepdims=True))
        total = jnp.zeros((MB, 1), f32)
        acc = jnp.zeros((MB, LAT), f32)
        for n in range(NB):
            p = jnp.exp(sc(n)[...] - top)
            total = total + jnp.sum(p, axis=1, keepdims=True)
            acc = acc + nn(p.astype(bf16), kbuf[n * SN : (n + 1) * SN, 0:LAT])
        qbuf[r, 0:LAT] = (acc / total).astype(bf16)

    each(0, H // 2, attend)

    from_z(lambda p: remote(zm.at[p], zm.at[p], zm_ss.at[p], zm_rs.at[p], {"tp": p}).wait_recv())
    lane = lax.broadcasted_iota(jnp.int32, (NT, NS), 1)
    wanted = (lax.div(lane, SL) * T + t).astype(f32)

    def hit(k):
        return (zm[...].reshape(NT, LANES)[:, k : k + 1] == wanted).astype(f32)

    m = zm[...].reshape(NT, LANES)
    total = m[:, K : K + 1]
    for k in range(1, K):
        total = total + m[:, K + k : K + k + 1]
    match = hit(0)
    weight = match * (route_scale * m[:, K : K + 1] / total)
    for k in range(1, K):
        h_ = hit(k)
        match = match + h_
        weight = weight + h_ * (route_scale * m[:, K + k : K + k + 1] / total)
    below = (
        lax.broadcasted_iota(jnp.int32, (NT, NT), 1) < lax.broadcasted_iota(jnp.int32, (NT, NT), 0)
    ).astype(bf16)
    rank = nn(below, match.astype(bf16))
    pick = jnp.where(rank == lax.rem(lane, SL).astype(f32), match, 0.0)
    place[...] = pick.astype(bf16)
    weight = weight * pick
    w_hi = weight.astype(bf16)
    wts[0] = w_hi
    wts[1] = (weight - w_hi.astype(f32)).astype(bf16)

    from_z(lambda p: remote(zg.at[p], zg.at[p], zg_ss.at[p], zg_rs.at[p], {"tp": p}).wait_recv())

    def g_cols(n):
        return pl.ds(pl.multiple_of(n * CG, CG), CG)

    def place_g(n):
        cols = g_cols(n)
        sx[:, :, cols] = tn(place[...], zg[:, :, cols].reshape(NT, CG)).astype(bf16).reshape(C, SL, CG)
        ag[c, :, cols] = sx[c, :, cols]

    each(0, 2, place_g)

    def relay(bo_):
        def one(ai):
            owner = lax.rem(a + ai, NX) * sa + lax.rem(b + NX - bo_, NX) * sb
            wait_recv(vo(owner, 0, owner))
            start(vo_relay(owner, d))

        each(0, NX, one)

    for o in (1, 3, 2) if NX == 4 else range(1, NX):
        relay(o)

    def xg(n, p, q):
        cols = g_cols(n)
        return remote(sx.at[p, :, cols], ag.at[q, :, cols], xg_ss.at[n, p], xg_rs.at[n, q], {"ctx": p})

    each(0, 2, lambda n: to_xy(lambda p: xg(n, p, c).start()))

    from_xy(lambda p: wait_recv(vo_relay(p, 1 - d)))
    swap_d.start()
    swap_u.start()

    for h in range(H):
        heads[:, h * VD : (h + 1) * VD] = nn(qbuf[h * rows : (h + 1) * rows, 0:LAT], vbuf[h]).astype(bf16)

    def u_cols(n):
        return pl.ds(pl.multiple_of(n * CD, CD), CD)

    def partial(n, p, q):
        cols = u_cols(n)
        return remote(part.at[p, :, cols], rsb.at[q, :, cols], r_ss.at[n, p], r_rs.at[n, q], {"tp": p})

    def project(n):
        cols = u_cols(n)
        part[:, :, cols] = nt(heads[...], obuf[cols, :]).astype(bf16).reshape(T, tok, CD)
        to_z(lambda p: partial(n, p, t).start())
        rsb[t, :, cols] = part[t, :, cols]

    each(0, ND, project)

    def sent_vo(off):
        for o in range(1, NX):
            wait_send(vo(c, NX * off + o, c))

    each(0, NX + 1, sent_vo)
    from_xy(lambda p: wait_send(vo_relay(p, d)))
    pl.semaphore_signal(ready, inc=1, device_id=sib, device_id_type=MESH)
    own_g.start()

    each(0, ND, lambda n: from_z(lambda p: partial(n, p, p).wait_recv()))
    hs = rsb[0].astype(f32)
    for i in range(1, T):
        hs = hs + rsb[i].astype(f32)
    hs = hs + res[...].astype(f32)
    hs_o[...] = hs
    inv = lax.rsqrt(jnp.mean(hs * hs, axis=1, keepdims=True) + norm_eps)
    zu[t] = (hs * inv * row_of(gain)).astype(bf16)

    def z_u(n, p, q):
        cols = u_cols(n)
        return remote(zu.at[q, :, cols], zu.at[q, :, cols], zu_ss.at[n, p], zu_rs.at[n, q], {"tp": p})

    each(0, ND, lambda n: to_z(lambda p: z_u(n, p, t).start()))
    pl.semaphore_wait(ready, 1)
    swap_g.start()
    each(0, 2, lambda n: from_xy(lambda p: xg(n, p, c).wait_send()))

    def x_u(n, p, q):
        cols = u_cols(n)
        return remote(sx.at[p, :, cols], au.at[q, :, cols], xu_ss.at[n, p], xu_rs.at[n, q], {"ctx": p})

    def send_u(n):
        cols = u_cols(n)
        from_z(lambda p: z_u(n, p, p).wait_recv())
        sx[:, :, cols] = tn(place[...], zu[:, :, cols].reshape(NT, CD)).astype(bf16).reshape(C, SL, CD)
        to_xy(lambda p: x_u(n, p, c).start())
        au[c, :, cols] = sx[c, :, cols]

    each(0, ND, send_u)

    own_d.wait()
    swap_d.wait()
    act[2] = jnp.zeros((NS, HID), f32)

    def d_hidden(n):
        from_xy(lambda p: xg(n, p, p).wait_recv())
        cols = g_cols(n)
        act[2] += nt(ag[:, :, cols].reshape(NS, CG), ds_[:, cols])

    each(0, 2, d_hidden)
    own_u.wait()
    swap_u.wait()
    own_g.wait()
    swap_g.wait()
    act[0] = jnp.zeros((NS, HID), f32)
    act[1] = jnp.zeros((NS, HID), f32)

    def gate_up(n):
        from_xy(lambda p: x_u(n, p, p).wait_recv())
        cols = u_cols(n)
        x = au[:, :, cols].reshape(NS, CD)
        act[0] += nn(x, gs[cols, :])
        act[1] += nn(x, us[cols, :])

    each(0, ND, gate_up)

    EB = NS // 4

    def pointwise(i):
        r = pl.ds(pl.multiple_of(i * EB, EB), EB)
        a_, b_, dh = act[0, r, :], act[1, r, :], act[2, r, :]
        sig = jax.nn.sigmoid(a_)
        gated = a_ * sig
        ab[0, r, :] = (gated * b_).astype(bf16)
        ab[1, r, :] = (dh * b_ * (sig * (1.0 + a_ * (1.0 - sig)))).astype(bf16)
        ab[2, r, :] = (dh * gated).astype(bf16)

    each(0, 4, pointwise)

    backs = ((ro, bo), (rd, bd))

    def r_cols(n):
        return pl.ds(pl.multiple_of(n * CR, CR), CR)

    def back(i, n, p, q):
        s_, r_ = backs[i]
        cols = r_cols(n)
        return remote(s_.at[p, :, cols], r_.at[q, :, cols], b_ss.at[i * NR + n, p], b_rs.at[i * NR + n, q], {"ctx": p})

    def w_back(p, q):
        return remote(rw.at[p], bw.at[q], bw_ss.at[p], bw_rs.at[q], {"ctx": p})

    def result(n, wg):
        cols = r_cols(n)
        y = nn(ab[0], ds_[:, cols]).astype(bf16)
        ro[:, :, cols] = y.reshape(C, SL, CR)
        to_xy(lambda p: back(0, n, p, c).start())
        bo[c, :, cols] = ro[c, :, cols]
        return wg + jnp.sum(y.astype(f32) * ag[:, :, cols].reshape(NS, CR).astype(f32), axis=1, keepdims=True)

    wg = lax.fori_loop(0, NR, result, jnp.zeros((NS, 1), f32))
    rw[...] = jnp.broadcast_to(wg, (NS, LANES)).reshape(rw.shape)
    to_xy(lambda p: w_back(p, c).start())
    bw[c] = rw[c]

    def grads(n):
        cols = r_cols(n)
        y = nt(ab[1], gs[cols, :]) + nt(ab[2], us[cols, :])
        rd[:, :, cols] = y.astype(bf16).reshape(C, SL, CR)
        to_xy(lambda p: back(1, n, p, c).start())
        bd[c, :, cols] = rd[c, :, cols]

    each(0, NR, grads)

    each(0, ND, lambda n: to_z(lambda p: partial(n, p, t).wait_send()))
    sums = ((part, fo), (pd, fd))

    def z_back(i, n, p, q):
        s_, r_ = sums[i]
        cols = r_cols(n)
        return remote(s_.at[p, :, cols], r_.at[q, :, cols], y_ss.at[i * NR + n, p], y_rs.at[i * NR + n, q], {"tp": p})

    def w_sum(p, q):
        return remote(pw.at[p], fw.at[q], yw_ss.at[p], yw_rs.at[q], {"tp": p})

    def combine(i):
        def chunk(n):
            cols = r_cols(n)
            from_xy(lambda p: back(i, n, p, p).wait_recv())
            x = backs[i][1][:, :, cols].reshape(NS, CR)
            sums[i][0][:, :, cols] = (nn(wts[0], x) + nn(wts[1], x)).astype(bf16).reshape(T, tok, CR)
            to_z(lambda p: z_back(i, n, p, t).start())
            sums[i][1][t, :, cols] = sums[i][0][t, :, cols]

        each(0, NR, chunk)

    combine(0)
    from_xy(lambda p: w_back(p, p).wait_recv())
    wcol = bw[...].reshape(NS, LANES)
    wlane = lax.broadcasted_iota(jnp.int32, (NT, LANES), 1)
    wgk = jnp.zeros((NT, LANES), f32)
    chosen = place[...].astype(f32)
    for k in range(K):
        v = lax.dot_general(
            hit(k) * chosen, wcol, (((1,), (0,)), ((), ())), preferred_element_type=f32, precision=lax.Precision.HIGHEST
        )
        wgk = jnp.where(wlane == k, v, wgk)
    pw[...] = wgk.reshape(pw.shape)
    to_z(lambda p: w_sum(p, t).start())
    fw[t] = pw[t]
    combine(1)

    def total_of(ref):
        v = ref[0].astype(f32)
        for i in range(1, T):
            v = v + ref[i].astype(f32)
        return v

    each(0, NR, lambda n: from_z(lambda p: z_back(0, n, p, p).wait_recv()))
    so_o[...] = total_of(fo)
    from_z(lambda p: w_sum(p, p).wait_recv())
    wg_o[...] = total_of(fw)

    to_z(lambda p: remote(zm.at[t], zm.at[t], zm_ss.at[p], zm_rs.at[t], {"tp": p}).wait_send())
    to_z(lambda p: remote(zg.at[t], zg.at[t], zg_ss.at[p], zg_rs.at[t], {"tp": p}).wait_send())
    each(0, ND, lambda n: to_z(lambda p: z_u(n, p, t).wait_send()))
    each(0, ND, lambda n: from_xy(lambda p: x_u(n, p, c).wait_send()))
    for i in range(2):
        each(0, NR, lambda n: from_xy(lambda p: back(i, n, p, c).wait_send()))
    from_xy(lambda p: w_back(p, c).wait_send())
    first_hops(lambda x: x.wait_send())
    for i in range(NX):
        second_hops(i, lambda x: x.wait_send())

    each(0, NR, lambda n: from_z(lambda p: z_back(1, n, p, p).wait_recv()))
    dn_o[...] = total_of(fd)
    to_z(lambda p: w_sum(p, t).wait_send())
    for i in range(2):
        each(0, NR, lambda n: to_z(lambda p: z_back(i, n, p, t).wait_send()))


def final_kernel(K, hs, so, dn, wg, g, sct, gain, lo_o, rg_o, sg_o):
    h = hs[...]
    lo_o[...] = (h + so[...]).astype(bf16)
    wgt = exact_nt(unit_rows(K, 0), wg[...])
    sc = sct[...]
    st = jnp.sum(sc, axis=0, keepdims=True)
    sg_o[...] = route_scale / st * (wgt - jnp.sum(wgt * sc, axis=0, keepdims=True) / st)
    dng = dn[...] * row_of(gain)
    inv = lax.rsqrt(jnp.mean(h * h, axis=1, keepdims=True) + norm_eps)
    proj = jnp.mean(dng * h, axis=1, keepdims=True)
    rg_o[...] = (g[...].astype(f32) + inv * dng - h * (inv * inv * inv * proj)).astype(bf16)


VM = pl.BlockSpec(memory_space=pltpu.VMEM)
ANY = pl.BlockSpec(memory_space=pl.ANY)


def per_device(
    C, T,
    query_latent, query_rotary, key_latent, key_rotary, value_up, out_proj, residual, norm_gain,
    gate_proj, up_proj, down_proj, expert_ids, route_score, out_grad,
):
    rows = query_latent.shape[1]
    H, LR, VD = value_up.shape
    LAT, ROPE = key_latent.shape[2], key_rotary.shape[2]
    KW = LAT + LANES
    tok, D = residual.shape[1:]
    K = expert_ids.shape[2]
    HID = gate_proj.shape[2]
    SL = CAP * T
    NS = C * SL
    NT = T * tok
    NX = math.isqrt(C)
    ND, NR = (7, 7) if D % (7 * LANES) == 0 else (4, 4)
    gain = norm_gain.reshape(D // LANES, LANES)
    id_t = jnp.swapaxes(expert_ids[0], 0, 1)
    score_t = jnp.swapaxes(route_score[0], 0, 1)
    dma = pltpu.SemaphoreType.DMA
    shape = jax.ShapeDtypeStruct
    vmem = pltpu.VMEM
    xy = (C, SL, D)
    zz = (T, tok, D)

    hs, so, dn, wg = pl.pallas_call(
        functools.partial(main_kernel, C, T, K, ND, NR),
        name="layer",
        out_shape=(shape((tok, D), f32), shape((tok, D), f32), shape((tok, D), f32), shape((tok, LANES), f32)),
        in_specs=[VM] * 11 + [ANY] * 3,
        out_specs=(VM,) * 4,
        scratch_shapes=[
            vmem((H * rows, KW), bf16),
            vmem((C * rows, KW), bf16),
            vmem((H, LAT, VD), bf16),
            vmem((D, H * VD), bf16),
            vmem((D, HID), bf16),
            vmem((HID, D), bf16),
            vmem((rows, H * VD), bf16),
            vmem(zz, bf16), vmem(zz, bf16),
            vmem((T, tok, LANES), f32), vmem(zz, bf16), vmem(zz, bf16),
            vmem(xy, bf16), vmem(xy, bf16), vmem(xy, bf16),
            vmem((3, NS, HID), f32),
            vmem((3, NS, HID), bf16),
            vmem((NT, NS), bf16), vmem((2, NT, NS), bf16),
            vmem(xy, bf16), vmem(xy, bf16), vmem((C, SL, LANES), f32),
            vmem(xy, bf16), vmem(xy, bf16), vmem((C, SL, LANES), f32),
            vmem(zz, bf16), vmem((T, tok, LANES), f32),
            vmem(zz, bf16), vmem(zz, bf16), vmem((T, tok, LANES), f32),
            dma((3,)), dma((3,)), dma((3,)),
            dma((NX * (NX + 1),)), dma((C,)),
            dma((NX * (NX + 1),)), dma((C,)), dma((NX * (NX + 1),)), dma((C,)),
            dma((C,)), dma((C,)), dma((C,)), dma((C,)),
            dma((ND, T)), dma((ND, T)),
            dma((T,)), dma((T,)), dma((T,)), dma((T,)), dma((ND, T)), dma((ND, T)),
            dma((2, C)), dma((2, C)), dma((ND, C)), dma((ND, C)),
            dma((2 * NR, C)), dma((2 * NR, C)), dma((C,)), dma((C,)),
            dma((2 * NR, T)), dma((2 * NR, T)), dma((T,)), dma((T,)),
            pltpu.SemaphoreType.REGULAR,
        ],
        compiler_params=pltpu.CompilerParams(
            collective_id=0, has_side_effects=True, vmem_limit_bytes=60 * 1024 * 1024
        ),
    )(
        query_latent[0], query_rotary[0], key_latent[0], jnp.swapaxes(key_rotary[0], 0, 1), value_up,
        jnp.swapaxes(out_proj, 1, 2), residual[0], gain, out_grad[0], id_t, score_t, gate_proj[0], up_proj[0],
        down_proj[0],
    )
    layer_out, resid_grad, score_grad = pl.pallas_call(
        functools.partial(final_kernel, K),
        name="finish",
        out_shape=(shape((tok, D), bf16), shape((tok, D), bf16), shape((K, tok), f32)),
        in_specs=[VM] * 7,
        out_specs=(VM,) * 3,
    )(hs, so, dn, wg, out_grad[0], score_t, gain)
    return (layer_out[None], resid_grad[None], jnp.swapaxes(score_grad, 0, 1)[None])


def solution(mesh):
    return jax.shard_map(
        functools.partial(per_device, mesh.shape["ctx"], mesh.shape["tp"]),
        mesh=mesh,
        in_specs=(
            P("dp", "ctx", "tp"),
            P("dp", "ctx", "tp"),
            P("dp", "ctx", None),
            P("dp", "ctx", None),
            P("tp", "ctx", None),
            P("tp", None, "ctx"),
            P("dp", ("ctx", "tp"), None),
            P(),
            P(("ctx", "tp"), "dp", None),
            P(("ctx", "tp"), "dp", None),
            P(("ctx", "tp"), "dp", None),
            P("dp", ("ctx", "tp"), None),
            P("dp", ("ctx", "tp"), None),
            P("dp", ("ctx", "tp"), None),
        ),
        out_specs=(
            P("dp", ("ctx", "tp"), None),
            P("dp", ("ctx", "tp"), None),
            P("dp", ("ctx", "tp"), None),
        ),
        check_vma=False,
    )
```
